256 devices in a mesh: pages: 64 (over x, z, core), query: 4 (over y).
Axes of the slice: x: 4, y: 4, z: 8, core: 2. Of those that a mesh axis runs over, the one named last changes fastest.
Arguments:
- queries: bfloat16 [64, 48, 32, 128], P('pages', 'query'), may hold values from -8 to 8
- pages: bfloat16 [1024, 1024, 128], P('pages', 'query'), may hold values from -8 to 8
- cand_owner: int32 [64, 24], P('pages'), may hold values from 0 to 63, all different within a row
- cand_slot: int32 [64, 24], P('pages'), may hold values from 0 to 15
Outputs:
- losses: float32 [64, 48], P('pages', 'query')
- query_grad: float32 [64, 48, 32, 128], P('pages', 'query')
- page_grad: float32 [1024, 1024, 128], P('pages', 'query')
The draws below stay inside these ranges and needn't reach their ends.
Inputs may be any that keep to these rules, and one draw needn't show every extreme that they name: `cand_owner`: each row names 24 different owner indices, and every index is named by some row.
All inputs are finite; a program needn't handle non-finite values.
Results may differ from the reference program's by a relative error of at most 0.0024.
Values may be sent and summed in bfloat16 or wider, within the bound.
No kernel may reach another device: no remote copies, remote signals or barrier semaphores. Data moves between devices by JAX's collectives and lax.ppermute only.
A program may use at most 64 MiB of HBM per device.

```python
import jax
import jax.numpy as jnp
from jax import lax

E = 128
PATCHES = 1024
QB = 48
QT = 32
PG_DEV = 16
C = 24
NB = 64
NPAGE = 1024
N_PAGES = 64


def shared_direction(key):
    direction = jax.random.normal(jax.random.fold_in(key, 7101), (E,), jnp.float32)
    return direction / jnp.sqrt(jnp.sum(direction * direction))


def draw_queries(key, part):
    direction = shared_direction(key)
    shape = (NB, QB, QT, E)
    noise_key = jax.random.fold_in(key, 211)
    level_key = jax.random.fold_in(key, 223)
    token_key = jax.random.fold_in(key, 227)
    noise = jnp.clip(jax.random.normal(noise_key, shape, jnp.float32), -4.0, 4.0)
    query_level = jax.random.uniform(level_key, (NB, QB, 1, 1), jnp.float32, 0.3, 1.1)
    token_level = jax.random.uniform(token_key, (NB, QB, QT, 1), jnp.float32, 0.5, 1.5)
    values = noise + query_level * token_level * E ** 0.5 * direction
    return jnp.clip(values, -8.0, 8.0).astype(jnp.bfloat16)


def draw_pages(key, part):
    direction = shared_direction(key)
    shape = (NPAGE, PATCHES, E)
    noise_key = jax.random.fold_in(key, 307)
    level_key = jax.random.fold_in(key, 311)
    patch_key = jax.random.fold_in(key, 313)
    noise = jnp.clip(jax.random.normal(noise_key, shape, jnp.float32), -4.0, 4.0)
    page_level = jax.random.uniform(level_key, (NPAGE, 1, 1), jnp.float32, 0.0, 0.9)
    patch_level = jax.random.uniform(patch_key, (NPAGE, PATCHES, 1), jnp.float32, 0.3, 1.7)
    values = noise + page_level * patch_level * E ** 0.5 * direction
    return jnp.clip(values, -8.0, 8.0).astype(jnp.bfloat16)


def touch_ends(values, key, least, top_value):
    index_at = [jax.random.randint(jax.random.fold_in(key, axis), (), 0, length) for axis, length in enumerate(values.shape)]
    main_axis = values.shape.index(max(values.shape))
    next_to = index_at[:main_axis] + [(index_at[main_axis] + 1) % values.shape[main_axis]] + index_at[main_axis + 1:]
    return values.at[tuple(index_at)].set(least).at[tuple(next_to)].set(top_value)


def choose_distinct(own_key, rows, number_of, top, lift):
    order = jax.random.permutation(jax.random.fold_in(own_key, 1), number_of)
    boost = order
    for power in range(3):
        boost = boost * boost // number_of
    boost = boost * lift // number_of
    lots = jax.random.randint(jax.random.fold_in(own_key, 2), (rows, number_of), 0, 4096) + boost
    sure = jax.random.permutation(jax.random.fold_in(own_key, 3), rows)[jnp.arange(number_of) % rows]
    lots = jnp.where(jnp.arange(rows)[:, None] == sure[None, :], 1 << 14, lots)
    merit = lots * number_of + jnp.arange(number_of)
    return lax.top_k(merit.astype(jnp.int32), top)[1].astype(jnp.int32)


def setup_inputs(seed: int = 0) -> dict:
    seeds = jax.random.split(jax.random.key(seed), 5)
    queries = draw_queries(jax.random.fold_in(seeds[4], 71), 0)
    pages = draw_pages(jax.random.fold_in(seeds[4], 71), 0)
    cand_owner = choose_distinct(seeds[2], NB, N_PAGES, C, 6144)
    cand_slot = touch_ends(jax.random.randint(seeds[3], (NB, C), 0, PG_DEV), jax.random.fold_in(seeds[3], 1), 0, PG_DEV - 1).astype(jnp.int32)
    return {"queries": queries, "pages": pages, "cand_owner": cand_owner, "cand_slot": cand_slot}


SHARPNESS = 10.0
INV_TEMP = 20.0
LOSS_SCALE = 256.0
EPSILON = 1e-06

def normalize(embeddings):
    values = embeddings.astype(jnp.float32)
    inverse = lax.rsqrt(lax.optimization_barrier(jnp.sum(values * values, axis=-1, keepdims=True)) + EPSILON)
    return (values * inverse, inverse)

def unnormalize_grad(unit_vectors, inverse, gradient):
    return inverse * (gradient - unit_vectors * lax.optimization_barrier(jnp.sum(unit_vectors * gradient, axis=-1, keepdims=True)))

def coefficients(totals, tokens):
    candidates = totals.shape[0]
    queries_here = totals.shape[1] // tokens
    shaped = totals.reshape(candidates, queries_here, tokens)
    per_token = jnp.log(shaped) / SHARPNESS
    logits = INV_TEMP * lax.optimization_barrier(jnp.mean(per_token, axis=2))
    exponentials = jnp.exp(logits)
    denominator = lax.optimization_barrier(jnp.sum(exponentials, axis=0))
    losses = jnp.log(denominator) - logits[0]
    positive = (jnp.arange(candidates) == 0).astype(jnp.float32)[:, None]
    probability = exponentials / denominator
    scaled = LOSS_SCALE * INV_TEMP / tokens * (probability - positive)
    weights = scaled[:, :, None] / shaped
    return (weights.reshape(candidates, queries_here * tokens), losses)

def reference(queries, pages, cand_owner, cand_slot):
    q_unit, q_inv = normalize(queries)
    d_unit, d_inv = normalize(pages)
    q_round = q_unit.astype(jnp.bfloat16)
    d_round = d_unit.astype(jnp.bfloat16)
    page_id = (cand_owner * PG_DEV + cand_slot).astype(jnp.int32)

    def one_block(page_back, element):
        block_tokens, identities = element
        query_rows = block_tokens.reshape(QB * QT, E)
        chosen = jnp.take(d_round, identities, axis=0)

        def forward(unused, page_piece):
            scores = jnp.dot(query_rows, page_piece.T, preferred_element_type=jnp.float32)
            return (unused, lax.optimization_barrier(jnp.sum(jnp.exp(SHARPNESS * scores), axis=1)))
        _, totals = lax.scan(forward, None, chosen)
        weights, losses = coefficients(totals, QT)

        def backward(grad_rows, pair):
            page_piece, weight_row = pair
            scores = jnp.dot(query_rows, page_piece.T, preferred_element_type=jnp.float32)
            shares = (weight_row[:, None] * jnp.exp(SHARPNESS * scores)).astype(jnp.bfloat16)
            grad_rows = grad_rows + jnp.dot(shares, page_piece, preferred_element_type=jnp.float32)
            page_term = jnp.dot(shares.T, query_rows, preferred_element_type=jnp.float32)
            return (grad_rows, page_term)
        grad_rows, page_terms = lax.scan(backward, jnp.zeros((QB * QT, E), jnp.float32), (chosen, weights))
        page_back = page_back.at[identities].add(page_terms)
        return (page_back, (grad_rows.reshape(QB, QT, E), losses))
    start = jnp.zeros(pages.shape, jnp.float32)
    page_back, (query_back, losses) = lax.scan(one_block, start, (q_round, page_id))
    query_grad = unnormalize_grad(q_unit, q_inv, query_back)
    page_grad = unnormalize_grad(d_unit, d_inv, page_back)
    return (losses, query_grad, page_grad)
```

```python
import functools
import math

import jax
import jax.numpy as jnp
from jax import lax
from jax.experimental import pallas as pl
from jax.experimental.pallas import tpu as pltpu
from jax.sharding import PartitionSpec as P

SHARPNESS = 10.0
INV_TEMP = 20.0
LOSS_SCALE = 256.0
EPSILON = 1e-06
EXP2_SCALE = SHARPNESS * math.log2(math.e)
PER_STEP = 4
GRAD_TYPE = jnp.bfloat16
OWN_TYPE = jnp.bfloat16


def exchange(value, axis):
    return lax.all_to_all(value, axis, split_axis=0, concat_axis=0, tiled=True)


def from_everyone(value, axis):
    devices = lax.axis_size(axis)
    return exchange(jnp.broadcast_to(value[None], (devices, *value.shape)), axis)


def normalize(embeddings):
    values = embeddings.astype(jnp.float32)
    inverse = lax.rsqrt(jnp.sum(values * values, axis=-1, keepdims=True) + EPSILON)
    return (values * inverse, inverse)


def unnormalize_grad(unit_vectors, inverse, gradient):
    return inverse * (
        gradient - unit_vectors * jnp.sum(unit_vectors * gradient, axis=-1, keepdims=True)
    )


def coefficients(totals, tokens):
    candidates = totals.shape[0]
    queries_here = totals.shape[1] // tokens
    shaped = totals.reshape(candidates, queries_here, tokens)
    per_token = jnp.log(shaped) / SHARPNESS
    logits = INV_TEMP * jnp.mean(per_token, axis=2)
    exponentials = jnp.exp(logits)
    denominator = jnp.sum(exponentials, axis=0)
    losses = jnp.log(denominator) - logits[0]
    positive = (jnp.arange(candidates) == 0).astype(jnp.float32)[:, None]
    probability = exponentials / denominator
    scaled = LOSS_SCALE * INV_TEMP / tokens * (probability - positive)
    weights = scaled[:, :, None] / shaped
    return (weights.reshape(candidates, queries_here * tokens), losses)


def patches_of(block, width):
    pieces = block.shape[1] // width
    return jnp.concatenate([block[:, j * width : (j + 1) * width] for j in range(pieces)], axis=0)


def row_chunk(rows):
    return 256 if rows % 256 == 0 else rows


def forward_kernel(width, q_ref, page_ref, totals_ref, unit_ref):
    per_step, pieces = page_ref.shape[0], page_ref.shape[1]
    patches = pieces * page_ref.shape[2] // width
    rows = q_ref.shape[0]
    chunk = row_chunk(rows)
    for c in range(per_step):
        unit, _ = normalize(patches_of(page_ref[c], width))
        unit_ref[c * patches : (c + 1) * patches, :] = unit.astype(jnp.bfloat16)
    for start in range(0, rows, chunk):
        block = q_ref[start : start + chunk, :]
        for c in range(per_step):
            scores = lax.dot_general(
                unit_ref[c * patches : (c + 1) * patches, :],
                block,
                (((1,), (1,)), ((), ())),
                preferred_element_type=jnp.float32,
            )
            sums = jnp.sum(jnp.exp2(scores * EXP2_SCALE), axis=0, keepdims=True)
            totals_ref[c, :, start : start + chunk] = sums


def backward_kernel(
    width, q_ref, page_ref, weight_ref, grad_ref, rows_ref, unit_ref, share_ref, back_ref
):
    per_step, pieces = page_ref.shape[0], page_ref.shape[1]
    patches = pieces * page_ref.shape[2] // width
    rows = q_ref.shape[0]
    chunk = row_chunk(rows)
    step = pl.program_id(0)
    for c in range(per_step):
        unit, _ = normalize(patches_of(page_ref[c], width))
        unit_ref[c * patches : (c + 1) * patches, :] = unit.astype(jnp.bfloat16)
    for start in range(0, rows, chunk):
        block = q_ref[start : start + chunk, :]
        for c in range(per_step):
            scores = lax.dot_general(
                unit_ref[c * patches : (c + 1) * patches, :],
                block,
                (((1,), (1,)), ((), ())),
                preferred_element_type=jnp.float32,
            )
            share = weight_ref[c, :, start : start + chunk] * jnp.exp2(scores * EXP2_SCALE)
            share_ref[c * patches : (c + 1) * patches, start : start + chunk] = share.astype(
                jnp.bfloat16
            )
    term = lax.dot_general(
        unit_ref[...], share_ref[...], (((0,), (0,)), ((), ())), preferred_element_type=jnp.float32
    )

    @pl.when(step == 0)
    def _():
        back_ref[...] = term

    @pl.when(step > 0)
    def _():
        back_ref[...] += term

    for c in range(per_step):
        gradient = jnp.dot(
            share_ref[c * patches : (c + 1) * patches, :],
            q_ref[...],
            preferred_element_type=jnp.float32,
        )
        unit, inverse = normalize(patches_of(page_ref[c], width))
        gradient = unnormalize_grad(unit, inverse, gradient).astype(grad_ref.dtype)
        for j in range(patches // pieces):
            grad_ref[c, :, j * width : (j + 1) * width] = gradient[j * pieces : (j + 1) * pieces, :]

    @pl.when(step == pl.num_programs(0) - 1)
    def _():
        rows_ref[...] = back_ref[...].T


def forward_totals(query_rows, chosen):
    rows, width = query_rows.shape
    candidates, pieces, wide = chosen.shape
    per_step = math.gcd(candidates, PER_STEP)
    patches = pieces * wide // width
    flops = 2 * candidates * patches * rows * width
    return pl.pallas_call(
        functools.partial(forward_kernel, width),
        grid=(candidates // per_step,),
        in_specs=[
            pl.BlockSpec((rows, width), lambda i: (0, 0)),
            pl.BlockSpec((per_step, pieces, wide), lambda i: (i, 0, 0)),
        ],
        out_specs=pl.BlockSpec((per_step, 1, rows), lambda i: (i, 0, 0)),
        out_shape=jax.ShapeDtypeStruct((candidates, 1, rows), jnp.float32),
        scratch_shapes=[pltpu.VMEM((per_step * patches, width), jnp.bfloat16)],
        cost_estimate=pl.CostEstimate(
            flops=flops,
            transcendentals=candidates * patches * rows,
            bytes_accessed=2 * candidates * patches * width,
        ),
        name="forward_totals",
    )(query_rows, chosen)


def backward_terms(query_rows, chosen, weights):
    rows, width = query_rows.shape
    candidates, pieces, wide = chosen.shape
    per_step = math.gcd(candidates, PER_STEP)
    patches = pieces * wide // width
    flops = 6 * candidates * patches * rows * width
    return pl.pallas_call(
        functools.partial(backward_kernel, width),
        grid=(candidates // per_step,),
        in_specs=[
            pl.BlockSpec((rows, width), lambda i: (0, 0)),
            pl.BlockSpec((per_step, pieces, wide), lambda i: (i, 0, 0)),
            pl.BlockSpec((per_step, 1, rows), lambda i: (i, 0, 0)),
        ],
        out_specs=[
            pl.BlockSpec((per_step, pieces, wide), lambda i: (i, 0, 0)),
            pl.BlockSpec((rows, width), lambda i: (0, 0)),
        ],
        out_shape=[
            jax.ShapeDtypeStruct(chosen.shape, GRAD_TYPE),
            jax.ShapeDtypeStruct((rows, width), jnp.float32),
        ],
        scratch_shapes=[
            pltpu.VMEM((per_step * patches, width), jnp.bfloat16),
            pltpu.VMEM((per_step * patches, rows), jnp.bfloat16),
            pltpu.VMEM((width, rows), jnp.float32),
        ],
        cost_estimate=pl.CostEstimate(
            flops=flops,
            transcendentals=candidates * patches * rows,
            bytes_accessed=4 * candidates * patches * width,
        ),
        name="backward_terms",
    )(query_rows, chosen, weights)


def local(queries, pages, cand_owner, cand_slot):
    queries_local, tokens, width = queries.shape[1:]
    local_pages, patches = pages.shape[:2]
    owners_count = lax.axis_size("pages")
    candidates = cand_owner.shape[1]
    rows_local = queries_local * tokens
    depth = patches // owners_count
    wide = depth * width
    pieces = pages.reshape(local_pages, depth, owners_count, width)
    spread = jnp.transpose(pieces, (2, 0, 1, 3)).reshape(owners_count, local_pages, wide)
    table = exchange(spread, "pages").reshape(owners_count * local_pages, wide)

    wanted = cand_owner[0] * local_pages + cand_slot[0]
    asked = from_everyone(wanted, "pages").reshape(owners_count * candidates)

    q_unit, q_inv = normalize(queries[0])
    q_round = q_unit.astype(jnp.bfloat16).reshape(rows_local, width)
    query_rows = from_everyone(q_round, "query").reshape(-1, width)

    page_range = jnp.arange(owners_count * local_pages, dtype=jnp.int32)
    picker = (asked[:, None] == page_range[None, :]).astype(jnp.bfloat16)
    served = jnp.dot(picker, table, preferred_element_type=jnp.float32).astype(jnp.bfloat16)
    fetched = exchange(served.reshape(owners_count, candidates, wide), "pages")
    chosen = jnp.transpose(fetched, (1, 0, 2))

    partial_totals = forward_totals(query_rows, chosen)
    totals = from_everyone(partial_totals.reshape(candidates, -1), "query").sum(axis=0)
    weights, losses_all = coefficients(totals, tokens)
    losses = lax.dynamic_slice_in_dim(
        losses_all, lax.axis_index("query") * queries_local, queries_local
    )

    page_terms, grad_rows = backward_terms(query_rows, chosen, weights[:, None, :])
    returned = exchange(jnp.transpose(page_terms, (1, 0, 2)), "pages")
    collector = (page_range[:, None] == asked[None, :]).astype(GRAD_TYPE)
    summed = jnp.dot(
        collector,
        returned.reshape(owners_count * candidates, wide),
        preferred_element_type=jnp.float32,
    )
    own = exchange(summed.astype(OWN_TYPE).reshape(owners_count, local_pages, wide), "pages")
    own = own.reshape(owners_count, local_pages, depth, width).astype(jnp.float32)
    page_grad = jnp.transpose(own, (1, 2, 0, 3)).reshape(pages.shape)

    own_grads = exchange(grad_rows.reshape(-1, rows_local, width), "query").sum(axis=0)
    query_grad = unnormalize_grad(
        q_unit, q_inv, own_grads.reshape(queries_local, tokens, width)
    )
    return (losses[None, :], query_grad[None], page_grad)


def solution(mesh):
    return jax.shard_map(
        local,
        mesh=mesh,
        in_specs=(
            P("pages", "query", None, None),
            P("pages", "query", None),
            P("pages", None),
            P("pages", None),
        ),
        out_specs=(P("pages", "query"), P("pages", "query", None, None), P("pages", "query", None)),
        check_vma=False,
    )
```

```python
import functools
import math

import jax
import jax.numpy as jnp
from jax import lax
from jax.experimental import pallas as pl
from jax.experimental.pallas import tpu as pltpu
from jax.sharding import PartitionSpec as P

SHARPNESS = 10.0
INV_TEMP = 20.0
LOSS_SCALE = 256.0
EPSILON = 1e-06
EXP2_SCALE = SHARPNESS * math.log2(math.e)
PER_STEP = 4
GRAD_TYPE = jnp.bfloat16
OWN_TYPE = jnp.bfloat16


def exchange(value, axis):
    return lax.all_to_all(value, axis, split_axis=0, concat_axis=0, tiled=True)


def normalize(embeddings):
    values = embeddings.astype(jnp.float32)
    inverse = lax.rsqrt(jnp.sum(values * values, axis=-1, keepdims=True) + EPSILON)
    return (values * inverse, inverse)


def unnormalize_grad(unit_vectors, inverse, gradient):
    return inverse * (
        gradient - unit_vectors * jnp.sum(unit_vectors * gradient, axis=-1, keepdims=True)
    )


def coefficients(totals, tokens):
    candidates = totals.shape[0]
    queries_here = totals.shape[1] // tokens
    shaped = totals.reshape(candidates, queries_here, tokens)
    per_token = jnp.log(shaped) / SHARPNESS
    logits = INV_TEMP * jnp.mean(per_token, axis=2)
    exponentials = jnp.exp(logits)
    denominator = jnp.sum(exponentials, axis=0)
    losses = jnp.log(denominator) - logits[0]
    positive = (jnp.arange(candidates) == 0).astype(jnp.float32)[:, None]
    probability = exponentials / denominator
    scaled = LOSS_SCALE * INV_TEMP / tokens * (probability - positive)
    weights = scaled[:, :, None] / shaped
    return (weights.reshape(candidates, queries_here * tokens), losses)


def patches_of(block, width):
    pieces = block.shape[1] // width
    return jnp.concatenate([block[:, j * width : (j + 1) * width] for j in range(pieces)], axis=0)


def row_chunk(rows):
    return 256 if rows % 256 == 0 else rows


def units_of(page_ref, unit_ref, width):
    patches = page_ref.shape[1] * page_ref.shape[2] // width
    for c in range(page_ref.shape[0]):
        unit, _ = normalize(patches_of(page_ref[c], width))
        unit_ref[c * patches : (c + 1) * patches, :] = unit.astype(jnp.bfloat16)
    return patches


def exponentials_of(unit_block, row_block):
    scores = lax.dot_general(
        unit_block, row_block, (((1,), (1,)), ((), ())), preferred_element_type=jnp.float32
    )
    return jnp.exp2(scores * EXP2_SCALE)


def forward_kernel(width, q_ref, page_ref, totals_ref, unit_ref):
    per_step = page_ref.shape[0]
    patches = units_of(page_ref, unit_ref, width)
    rows = q_ref.shape[0]
    chunk = row_chunk(rows)
    first = pl.program_id(0) * per_step
    for start in range(0, rows, chunk):
        block = q_ref[start : start + chunk, :]
        for c in range(per_step):
            values = exponentials_of(unit_ref[c * patches : (c + 1) * patches, :], block)
            totals_ref[pl.ds(first + c, 1), start : start + chunk] = jnp.sum(
                values, axis=0, keepdims=True
            )


def fill_shares(q_ref, weight_ref, unit_ref, share_ref, per_step, patches):
    rows = q_ref.shape[0]
    chunk = row_chunk(rows)
    first = pl.program_id(0) * per_step
    for start in range(0, rows, chunk):
        block = q_ref[start : start + chunk, :]
        for c in range(per_step):
            values = exponentials_of(unit_ref[c * patches : (c + 1) * patches, :], block)
            weight = weight_ref[pl.ds(first + c, 1), start : start + chunk]
            share_ref[c * patches : (c + 1) * patches, start : start + chunk] = (
                weight * values
            ).astype(jnp.bfloat16)


def page_side_kernel(width, q_ref, page_ref, weight_ref, grad_ref, unit_ref, share_ref):
    per_step, pieces = page_ref.shape[0], page_ref.shape[1]
    patches = units_of(page_ref, unit_ref, width)
    fill_shares(q_ref, weight_ref, unit_ref, share_ref, per_step, patches)
    for c in range(per_step):
        gradient = jnp.dot(
            share_ref[c * patches : (c + 1) * patches, :],
            q_ref[...],
            preferred_element_type=jnp.float32,
        )
        unit, inverse = normalize(patches_of(page_ref[c], width))
        gradient = unnormalize_grad(unit, inverse, gradient).astype(grad_ref.dtype)
        for j in range(patches // pieces):
            grad_ref[c, :, j * width : (j + 1) * width] = gradient[j * pieces : (j + 1) * pieces, :]


def query_side_kernel(width, q_ref, page_ref, weight_ref, rows_ref, unit_ref, share_ref, back_ref):
    per_step = page_ref.shape[0]
    patches = units_of(page_ref, unit_ref, width)
    fill_shares(q_ref, weight_ref, unit_ref, share_ref, per_step, patches)
    step = pl.program_id(0)
    term = lax.dot_general(
        unit_ref[...], share_ref[...], (((0,), (0,)), ((), ())), preferred_element_type=jnp.float32
    )

    @pl.when(step == 0)
    def _():
        back_ref[...] = term

    @pl.when(step > 0)
    def _():
        back_ref[...] += term

    @pl.when(step == pl.num_programs(0) - 1)
    def _():
        rows_ref[...] = back_ref[...].T


def over_candidates(kernel, name, products, query_rows, chosen, weights, out_spec, out_shape, scratch):
    rows, width = query_rows.shape
    candidates, pieces, wide = chosen.shape
    per_step = math.gcd(candidates, PER_STEP)
    patches = pieces * wide // width
    table = pl.BlockSpec((candidates, rows), lambda i: (0, 0))
    return pl.pallas_call(
        functools.partial(kernel, width),
        grid=(candidates // per_step,),
        in_specs=[
            pl.BlockSpec((rows, width), lambda i: (0, 0)),
            pl.BlockSpec((per_step, pieces, wide), lambda i: (i, 0, 0)),
        ]
        + ([table] if weights else []),
        out_specs=out_spec or table,
        out_shape=out_shape,
        scratch_shapes=[pltpu.VMEM((per_step * patches, width), jnp.bfloat16)] + scratch,
        cost_estimate=pl.CostEstimate(
            flops=2 * products * candidates * patches * rows * width,
            transcendentals=candidates * patches * rows,
            bytes_accessed=4 * candidates * patches * width,
        ),
        name=name,
    )(query_rows, chosen, *weights)


def forward_totals(query_rows, chosen):
    shape = jax.ShapeDtypeStruct((chosen.shape[0], query_rows.shape[0]), jnp.float32)
    return over_candidates(
        forward_kernel, "forward_totals", 1, query_rows, chosen, [], None, shape, []
    )


def share_scratch(query_rows, chosen):
    per_step = math.gcd(chosen.shape[0], PER_STEP)
    patches = chosen.shape[1] * chosen.shape[2] // query_rows.shape[1]
    return pltpu.VMEM((per_step * patches, query_rows.shape[0]), jnp.bfloat16)


def page_side(query_rows, chosen, weights):
    per_step = math.gcd(chosen.shape[0], PER_STEP)
    return over_candidates(
        page_side_kernel,
        "page_side",
        2,
        query_rows,
        chosen,
        [weights],
        pl.BlockSpec((per_step, *chosen.shape[1:]), lambda i: (i, 0, 0)),
        jax.ShapeDtypeStruct(chosen.shape, GRAD_TYPE),
        [share_scratch(query_rows, chosen)],
    )


def query_side(query_rows, chosen, weights):
    return over_candidates(
        query_side_kernel,
        "query_side",
        2,
        query_rows,
        chosen,
        [weights],
        pl.BlockSpec(query_rows.shape, lambda i: (0, 0)),
        jax.ShapeDtypeStruct(query_rows.shape, jnp.float32),
        [
            share_scratch(query_rows, chosen),
            pltpu.VMEM((query_rows.shape[1], query_rows.shape[0]), jnp.float32),
        ],
    )


def from_ahead(value, axis, shift):
    devices = lax.axis_size(axis)
    pairs = [((i + shift) % devices, i) for i in range(devices)]
    return lax.ppermute(value, axis, pairs)


def gathered(value, axis):
    devices = lax.axis_size(axis)
    me = lax.axis_index(axis)
    parts, stride = value[None], 1
    for factor in factors(devices):
        place = (me // stride) % factor
        received = [parts]
        for shift in range(1, factor):
            pairs = []
            for i in range(devices):
                ahead = (i // stride + shift) % factor
                pairs.append((i + (ahead - (i // stride) % factor) * stride, i))
            received.append(lax.ppermute(parts, axis, pairs))
        ahead_first = jnp.stack(received)
        ordered = jnp.roll(ahead_first, place, axis=0) if factor > 1 else ahead_first
        parts = ordered.reshape(-1, *value.shape)
        stride *= factor
    return parts


def factors(devices):
    return [f for f in (2, devices // 8, 4) if f > 1] if devices >= 16 else [devices]


def local(queries, pages, cand_owner, cand_slot):
    queries_local, tokens, width = queries.shape[1:]
    local_pages, patches = pages.shape[:2]
    owners_count = lax.axis_size("pages")
    group = lax.axis_size("query")
    candidates = cand_owner.shape[1]
    rows_local = queries_local * tokens
    depth = patches // owners_count
    wide = depth * width
    pieces = pages.reshape(local_pages, depth, owners_count, width)
    spread = jnp.transpose(pieces, (2, 0, 1, 3)).reshape(owners_count, local_pages, wide)
    table = exchange(spread, "pages").reshape(owners_count * local_pages, wide)

    wanted = cand_owner[0] * local_pages + cand_slot[0]
    asked = gathered(wanted, "pages").reshape(owners_count * candidates)

    q_unit, q_inv = normalize(queries[0])
    q_round = q_unit.astype(jnp.bfloat16).reshape(rows_local, width)
    query_rows = jnp.concatenate(
        [q_round] + [from_ahead(q_round, "query", k) for k in range(1, group)], axis=0
    )

    page_range = jnp.arange(owners_count * local_pages, dtype=jnp.int32)
    picker = (asked[:, None] == page_range[None, :]).astype(jnp.bfloat16)
    served = jnp.dot(picker, table, preferred_element_type=jnp.float32).astype(jnp.bfloat16)
    fetched = exchange(served.reshape(owners_count, candidates, wide), "pages")
    chosen = jnp.transpose(fetched, (1, 0, 2))

    partial_totals = forward_totals(query_rows, chosen)
    totals = partial_totals
    for k in range(1, group):
        theirs = from_ahead(partial_totals, "query", k)
        totals = totals + jnp.roll(theirs, k * rows_local, axis=1)
    weights, losses_all = coefficients(totals, tokens)
    losses = losses_all[:queries_local]

    page_terms = page_side(query_rows, chosen, weights)
    returned = exchange(jnp.transpose(page_terms, (1, 0, 2)), "pages")
    collector = (page_range[:, None] == asked[None, :]).astype(GRAD_TYPE)
    summed = jnp.dot(
        collector,
        returned.reshape(owners_count * candidates, wide),
        preferred_element_type=jnp.float32,
    )
    own = exchange(summed.astype(OWN_TYPE).reshape(owners_count, local_pages, wide), "pages")
    own = own.reshape(owners_count, local_pages, depth, width).astype(jnp.float32)
    page_grad = jnp.transpose(own, (1, 2, 0, 3)).reshape(pages.shape)

    grad_rows = query_side(query_rows, chosen, weights).reshape(group, rows_local, width)
    own_grads = grad_rows[0]
    for k in range(1, group):
        own_grads = own_grads + from_ahead(grad_rows[k], "query", group - k)
    query_grad = unnormalize_grad(
        q_unit, q_inv, own_grads.reshape(queries_local, tokens, width)
    )
    return (losses[None, :], query_grad[None], page_grad)


def solution(mesh):
    return jax.shard_map(
        local,
        mesh=mesh,
        in_specs=(
            P("pages", "query", None, None),
            P("pages", "query", None),
            P("pages", None),
            P("pages", None),
        ),
        out_specs=(P("pages", "query"), P("pages", "query", None, None), P("pages", "query", None)),
        check_vma=False,
    )
```

```python
import functools
import math

import jax
import jax.numpy as jnp
from jax import lax
from jax.experimental import pallas as pl
from jax.experimental.pallas import tpu as pltpu
from jax.sharding import PartitionSpec as P

SHARPNESS = 10.0
INV_TEMP = 20.0
LOSS_SCALE = 256.0
EPSILON = 1e-06
EXP2_SCALE = SHARPNESS * math.log2(math.e)
PER_STEP = 8
PER_LOOP = 4
GRAD_TYPE = jnp.bfloat16
OWN_TYPE = jnp.bfloat16


def exchange(value, axis):
    return lax.all_to_all(value, axis, split_axis=0, concat_axis=0, tiled=True)


def normalize(embeddings):
    values = embeddings.astype(jnp.float32)
    inverse = lax.rsqrt(jnp.sum(values * values, axis=-1, keepdims=True) + EPSILON)
    return (values * inverse, inverse)


def unnormalize_grad(unit_vectors, inverse, gradient):
    return inverse * (
        gradient - unit_vectors * jnp.sum(unit_vectors * gradient, axis=-1, keepdims=True)
    )


def coefficients(totals, tokens):
    candidates = totals.shape[0]
    queries_here = totals.shape[1] // tokens
    shaped = totals.reshape(candidates, queries_here, tokens)
    per_token = jnp.log(shaped) / SHARPNESS
    logits = INV_TEMP * jnp.mean(per_token, axis=2)
    exponentials = jnp.exp(logits)
    denominator = jnp.sum(exponentials, axis=0)
    losses = jnp.log(denominator) - logits[0]
    positive = (jnp.arange(candidates) == 0).astype(jnp.float32)[:, None]
    probability = exponentials / denominator
    scaled = LOSS_SCALE * INV_TEMP / tokens * (probability - positive)
    weights = scaled[:, :, None] / shaped
    return (weights.reshape(candidates, queries_here * tokens), losses)


def row_chunk(rows):
    return 256 if rows % 256 == 0 else rows


def load_pages(page_ref, raw_ref):
    pieces, per_step, _ = page_ref.shape
    depth, rows, width = raw_ref.shape
    for j in range(depth):
        block = page_ref[:, :, j * width : (j + 1) * width].astype(jnp.float32)
        raw_ref[j] = block.reshape(rows, width)


def candidate_rows(raw_ref, c, per_step):
    depth, rows, _ = raw_ref.shape
    parts = [raw_ref[j, pl.ds(c, rows // per_step, stride=per_step), :] for j in range(depth)]
    return jnp.concatenate(parts, axis=0)


def prepare(page_ref, raw_ref, unit_ref):
    per_step = page_ref.shape[1]
    load_pages(page_ref, raw_ref)
    patches = unit_ref.shape[0] // per_step
    for c in range(per_step):
        unit, _ = normalize(candidate_rows(raw_ref, c, per_step))
        unit_ref[c * patches : (c + 1) * patches, :] = unit.astype(jnp.bfloat16)
    return per_step, patches


def exponentials_of(unit_block, row_block):
    scores = lax.dot_general(
        unit_block, row_block, (((1,), (1,)), ((), ())), preferred_element_type=jnp.float32
    )
    return jnp.exp2(scores * EXP2_SCALE)


def patch_slice(c, patches):
    return pl.ds(pl.multiple_of(c * patches, patches), patches)


def forward_kernel(q_ref, page_ref, totals_ref, raw_ref, unit_ref):
    per_step, patches = prepare(page_ref, raw_ref, unit_ref)
    rows = q_ref.shape[0]
    chunk = row_chunk(rows)
    together = math.gcd(per_step, PER_LOOP)
    first = pl.program_id(0) * per_step

    @pl.loop(0, per_step // together)
    def _(turn):
        for start in range(0, rows, chunk):
            block = q_ref[start : start + chunk, :]
            for k in range(together):
                c = turn * together + k
                values = exponentials_of(unit_ref[patch_slice(c, patches), :], block)
                totals_ref[pl.ds(first + c, 1), start : start + chunk] = jnp.sum(
                    values, axis=0, keepdims=True
                )


def fill_shares(q_ref, weight_ref, unit_ref, share_ref, per_step, patches, turn):
    rows = q_ref.shape[0]
    chunk = row_chunk(rows)
    together = math.gcd(per_step, PER_LOOP)
    first = pl.program_id(0) * per_step
    for start in range(0, rows, chunk):
        block = q_ref[start : start + chunk, :]
        for k in range(together):
            c = turn * together + k
            values = exponentials_of(unit_ref[patch_slice(c, patches), :], block)
            weight = weight_ref[pl.ds(first + c, 1), start : start + chunk]
            share_ref[k * patches : (k + 1) * patches, start : start + chunk] = (
                weight * values
            ).astype(jnp.bfloat16)
    return together


def page_side_kernel(q_ref, page_ref, weight_ref, grad_ref, raw_ref, unit_ref, share_ref, back_ref):
    per_step, patches = prepare(page_ref, raw_ref, unit_ref)
    pieces = page_ref.shape[0]
    depth, _, width = raw_ref.shape

    @pl.loop(0, per_step // math.gcd(per_step, PER_LOOP))
    def _(turn):
        together = fill_shares(q_ref, weight_ref, unit_ref, share_ref, per_step, patches, turn)
        for k in range(together):
            back_ref[patch_slice(turn * together + k, patches), :] = jnp.dot(
                share_ref[k * patches : (k + 1) * patches, :],
                q_ref[...],
                preferred_element_type=jnp.float32,
            )

    for c in range(per_step):
        unit, inverse = normalize(candidate_rows(raw_ref, c, per_step))
        gradient = unnormalize_grad(unit, inverse, back_ref[c * patches : (c + 1) * patches, :])
        for j in range(depth):
            raw_ref[j, pl.ds(c, pieces, stride=per_step), :] = gradient[
                j * pieces : (j + 1) * pieces, :
            ]
    for j in range(depth):
        block = raw_ref[j].reshape(pieces, per_step, width)
        grad_ref[:, :, j * width : (j + 1) * width] = block.astype(grad_ref.dtype)


def query_side_kernel(
    q_ref, page_ref, weight_ref, rows_ref, raw_ref, unit_ref, share_ref, back_ref
):
    per_step, patches = prepare(page_ref, raw_ref, unit_ref)
    step = pl.program_id(0)

    @pl.when(step == 0)
    def _():
        back_ref[...] = jnp.zeros_like(back_ref)

    @pl.loop(0, per_step // math.gcd(per_step, PER_LOOP))
    def _(turn):
        together = fill_shares(q_ref, weight_ref, unit_ref, share_ref, per_step, patches, turn)
        back_ref[...] += lax.dot_general(
            unit_ref[patch_slice(turn, together * patches), :],
            share_ref[...],
            (((0,), (0,)), ((), ())),
            preferred_element_type=jnp.float32,
        )

    @pl.when(step == pl.num_programs(0) - 1)
    def _():
        rows_ref[...] = back_ref[...].T


def over_candidates(
    kernel, name, products, query_rows, fetched, weights, out_spec, out_shape, share, back
):
    rows, width = query_rows.shape
    pieces, candidates, wide = fetched.shape
    per_step = math.gcd(candidates, PER_STEP)
    patches = pieces * wide // width
    table = pl.BlockSpec((candidates, rows), lambda i: (0, 0))
    scratch = [
        pltpu.VMEM((wide // width, pieces * per_step, width), jnp.float32),
        pltpu.VMEM((per_step * patches, width), jnp.bfloat16),
    ]
    if share:
        together = math.gcd(per_step, PER_LOOP)
        scratch.append(pltpu.VMEM((together * patches, rows), jnp.bfloat16))
        scratch.append(pltpu.VMEM(back or (per_step * patches, width), jnp.float32))
    return pl.pallas_call(
        kernel,
        grid=(candidates // per_step,),
        in_specs=[
            pl.BlockSpec((rows, width), lambda i: (0, 0)),
            pl.BlockSpec((pieces, per_step, wide), lambda i: (0, i, 0)),
        ]
        + [table for _ in weights],
        out_specs=out_spec or table,
        out_shape=out_shape,
        scratch_shapes=scratch,
        cost_estimate=pl.CostEstimate(
            flops=2 * products * candidates * patches * rows * width,
            transcendentals=candidates * patches * rows,
            bytes_accessed=4 * candidates * patches * width,
        ),
        name=name,
    )(query_rows, fetched, *weights)


def forward_totals(query_rows, fetched):
    shape = jax.ShapeDtypeStruct((fetched.shape[1], query_rows.shape[0]), jnp.float32)
    return over_candidates(
        forward_kernel, "forward_totals", 1, query_rows, fetched, [], None, shape, False, None
    )


def page_side(query_rows, fetched, weights):
    pieces, candidates, wide = fetched.shape
    per_step = math.gcd(candidates, PER_STEP)
    spec = pl.BlockSpec((pieces, per_step, wide), lambda i: (0, i, 0))
    shape = jax.ShapeDtypeStruct(fetched.shape, GRAD_TYPE)
    return over_candidates(
        page_side_kernel, "page_side", 2, query_rows, fetched, [weights], spec, shape, True, None
    )


def query_side(query_rows, fetched, weights):
    spec = pl.BlockSpec(query_rows.shape, lambda i: (0, 0))
    shape = jax.ShapeDtypeStruct(query_rows.shape, jnp.float32)
    back = query_rows.shape[::-1]
    return over_candidates(
        query_side_kernel, "query_side", 2, query_rows, fetched, [weights], spec, shape, True, back
    )


def from_ahead(value, axis, shift):
    devices = lax.axis_size(axis)
    pairs = [((i + shift) % devices, i) for i in range(devices)]
    return lax.ppermute(value, axis, pairs)


ID_ROWS = 8


def local(queries, pages, cand_owner, cand_slot):
    queries_local, tokens, width = queries.shape[1:]
    local_pages, patches = pages.shape[:2]
    owners_count = lax.axis_size("pages")
    group = lax.axis_size("query")
    candidates = cand_owner.shape[1]
    rows_local = queries_local * tokens
    depth = patches // owners_count
    wide = depth * width
    pieces = pages.reshape(local_pages, depth, owners_count, width)
    spread = jnp.transpose(pieces, (2, 1, 0, 3)).reshape(owners_count, depth * local_pages, width)
    wanted = jnp.concatenate([cand_owner[0], cand_slot[0]]).astype(jnp.bfloat16)
    wanted = jnp.pad(wanted[None, :], ((0, ID_ROWS - 1), (0, width - 2 * candidates)))
    wanted = jnp.broadcast_to(wanted[None], (owners_count, ID_ROWS, width))
    arrived = exchange(jnp.concatenate([spread, wanted], axis=1), "pages")
    tiles = [arrived[:, j * local_pages : (j + 1) * local_pages, :] for j in range(depth)]
    table = jnp.concatenate(tiles, axis=2).reshape(owners_count * local_pages, wide)
    ids = arrived[:, depth * local_pages, : 2 * candidates].astype(jnp.int32)
    asked = ids[:, :candidates] * local_pages + ids[:, candidates:]
    asked = asked.reshape(owners_count * candidates)

    q_unit, q_inv = normalize(queries[0])
    q_round = q_unit.astype(jnp.bfloat16).reshape(rows_local, width)
    query_rows = jnp.concatenate(
        [q_round] + [from_ahead(q_round, "query", k) for k in range(1, group)], axis=0
    )

    page_range = jnp.arange(owners_count * local_pages, dtype=jnp.int32)
    picker = (asked[:, None] == page_range[None, :]).astype(jnp.bfloat16)
    served = jnp.dot(picker, table, preferred_element_type=jnp.float32).astype(jnp.bfloat16)
    fetched = exchange(served.reshape(owners_count, candidates, wide), "pages")

    partial_totals = forward_totals(query_rows, fetched)
    totals = partial_totals
    for k in range(1, group):
        theirs = from_ahead(partial_totals, "query", k)
        totals = totals + jnp.roll(theirs, k * rows_local, axis=1)
    weights, losses_all = coefficients(totals, tokens)
    losses = losses_all[:queries_local]

    returned = exchange(page_side(query_rows, fetched, weights), "pages")

    grad_rows = query_side(query_rows, fetched, weights).reshape(group, rows_local, width)
    own_grads = grad_rows[0]
    for k in range(1, group):
        own_grads = own_grads + from_ahead(grad_rows[k], "query", group - k)
    query_grad = unnormalize_grad(
        q_unit, q_inv, own_grads.reshape(queries_local, tokens, width)
    )
    returned, query_grad = lax.optimization_barrier((returned, query_grad))

    collector = (page_range[:, None] == asked[None, :]).astype(GRAD_TYPE)
    summed = jnp.dot(
        collector,
        returned.reshape(owners_count * candidates, wide),
        preferred_element_type=jnp.float32,
    )
    own = exchange(summed.astype(OWN_TYPE).reshape(owners_count, local_pages, wide), "pages")
    own = own.reshape(owners_count, local_pages, depth, width).astype(jnp.float32)
    page_grad = jnp.transpose(own, (1, 2, 0, 3)).reshape(pages.shape)
    return (losses[None, :], query_grad[None], page_grad)


def solution(mesh):
    return jax.shard_map(
        local,
        mesh=mesh,
        in_specs=(
            P("pages", "query", None, None),
            P("pages", "query", None),
            P("pages", None),
            P("pages", None),
        ),
        out_specs=(P("pages", "query"), P("pages", "query", None, None), P("pages", "query", None)),
        check_vma=False,
    )
```

```python
import functools
import math

import jax
import jax.numpy as jnp
from jax import lax
from jax.experimental import pallas as pl
from jax.experimental.pallas import tpu as pltpu
from jax.sharding import PartitionSpec as P

SHARPNESS = 10.0
INV_TEMP = 20.0
LOSS_SCALE = 256.0
EPSILON = 1e-06
EXP2_SCALE = SHARPNESS * math.log2(math.e)
PER_STEP = 8
PER_LOOP = 4
FIRST_CHUNK = 8
PARAMS = pltpu.CompilerParams(vmem_limit_bytes=24 << 20)
GRAD_TYPE = jnp.bfloat16
OWN_TYPE = jnp.bfloat16


def exchange(value, axis):
    return lax.all_to_all(value, axis, split_axis=0, concat_axis=0, tiled=True)


def normalize(embeddings):
    values = embeddings.astype(jnp.float32)
    inverse = lax.rsqrt(jnp.sum(values * values, axis=-1, keepdims=True) + EPSILON)
    return (values * inverse, inverse)


def unnormalize_grad(unit_vectors, inverse, gradient):
    return inverse * (
        gradient - unit_vectors * jnp.sum(unit_vectors * gradient, axis=-1, keepdims=True)
    )


def group_sums(values, size):
    lanes = values.shape[1]
    lane = lax.broadcasted_iota(jnp.int32, values.shape, 1)
    step = 1
    while step < size:
        ahead = pltpu.roll(values, lanes - step, 1)
        behind = pltpu.roll(values, step, 1)
        values = values + jnp.where((lane // step) % 2 == 0, ahead, behind)
        step *= 2
    return values


def weights_kernel(tokens, shifts, *refs):
    weight_ref, loss_ref = refs[-2:]
    rows = weight_ref.shape[1]
    group = len(shifts)
    tile = math.gcd(rows // group, 128)
    for start in range(0, rows, tile):
        totals = []
        for first in range(0, len(refs) - 2, group):
            total = None
            for ref, shift in zip(refs[first : first + group], shifts):
                at = (start - shift) % rows
                part = ref[:, at : at + tile]
                total = part if total is None else total + part
            totals.append(total)
        totals = jnp.concatenate(totals, axis=0)
        per_token = jnp.log(totals) / SHARPNESS
        logits = INV_TEMP * (group_sums(per_token, tokens) / tokens)
        exponentials = jnp.exp(logits)
        denominator = jnp.sum(exponentials, axis=0, keepdims=True)
        loss_ref[:, start : start + tile] = jnp.log(denominator) - logits[:1]
        candidate = lax.broadcasted_iota(jnp.int32, totals.shape, 0)
        positive = jnp.where(candidate == 0, 1.0, 0.0)
        scaled = LOSS_SCALE * INV_TEMP / tokens * (exponentials / denominator - positive)
        weight_ref[:, start : start + tile] = scaled / totals


def weights_of(chunks, shifts, tokens):
    rows = chunks[0][0].shape[1]
    candidates = sum(parts[0].shape[0] for parts in chunks)
    return pl.pallas_call(
        functools.partial(weights_kernel, tokens, shifts),
        out_shape=[
            jax.ShapeDtypeStruct((candidates, rows), jnp.float32),
            jax.ShapeDtypeStruct((1, rows), jnp.float32),
        ],
        compiler_params=PARAMS,
        name="weights",
    )(*[part for parts in chunks for part in parts])


def row_chunk(rows):
    return 256 if rows % 256 == 0 else rows


def load_pages(page_ref, raw_ref):
    pieces, per_step, _ = page_ref.shape
    depth, rows, width = raw_ref.shape
    for j in range(depth):
        block = page_ref[:, :, j * width : (j + 1) * width].astype(jnp.float32)
        raw_ref[j] = block.reshape(rows, width)


def candidate_rows(raw_ref, c, per_step):
    depth, rows, _ = raw_ref.shape
    parts = [raw_ref[j, pl.ds(c, rows // per_step, stride=per_step), :] for j in range(depth)]
    return jnp.concatenate(parts, axis=0)


def prepare(raw_ref, unit_ref, k, c, per_step):
    unit, inverse = normalize(candidate_rows(raw_ref, c, per_step))
    patches = unit.shape[0]
    unit_ref[k * patches : (k + 1) * patches, :] = unit.astype(jnp.bfloat16)
    return unit, inverse


def exponentials_of(unit_block, row_block):
    scores = lax.dot_general(
        unit_block, row_block, (((1,), (1,)), ((), ())), preferred_element_type=jnp.float32
    )
    return jnp.exp2(scores * EXP2_SCALE)


def fill(q_ref, raw_ref, unit_ref, turn, per_step, use):
    rows = q_ref.shape[0]
    chunk = row_chunk(rows)
    together = math.gcd(per_step, PER_LOOP)
    patches = unit_ref.shape[0] // together
    first = turn * together
    for k in range(together):
        prepare(raw_ref, unit_ref, k, first + k, per_step)
    for start in range(0, rows, chunk):
        block = q_ref[start : start + chunk, :]
        for k in range(together):
            values = exponentials_of(unit_ref[k * patches : (k + 1) * patches, :], block)
            use(k, patches, pl.ds(start, chunk), values)
    return together, patches, first


def share_into(share_ref, weight_ref, row):
    def use(k, patches, columns, values):
        share = weight_ref[pl.ds(row + k, 1), columns] * values
        share_ref[k * patches : (k + 1) * patches, columns] = share.astype(jnp.bfloat16)

    return use


def forward_kernel(q_ref, page_ref, totals_ref, raw_ref, unit_ref):
    per_step = page_ref.shape[1]
    load_pages(page_ref, raw_ref)
    step_first = pl.program_id(0) * per_step
    together = math.gcd(per_step, PER_LOOP)

    @pl.loop(0, per_step // together)
    def _(turn):
        def use(k, patches, columns, values):
            row = pl.ds(step_first + turn * together + k, 1)
            totals_ref[row, columns] = jnp.sum(values, axis=0, keepdims=True)

        fill(q_ref, raw_ref, unit_ref, turn, per_step, use)


def page_side_kernel(offset, q_ref, page_ref, weight_ref, grad_ref, raw_ref, unit_ref, share_ref):
    per_step = page_ref.shape[1]
    pieces = page_ref.shape[0]
    depth, _, width = raw_ref.shape
    load_pages(page_ref, raw_ref)
    step_first = offset + pl.program_id(0) * per_step

    @pl.loop(0, per_step // math.gcd(per_step, PER_LOOP))
    def _(turn):
        use = share_into(share_ref, weight_ref, step_first + turn * math.gcd(per_step, PER_LOOP))
        together, patches, first = fill(q_ref, raw_ref, unit_ref, turn, per_step, use)
        for k in range(together):
            gradient = jnp.dot(
                share_ref[k * patches : (k + 1) * patches, :],
                q_ref[...],
                preferred_element_type=jnp.float32,
            )
            unit, inverse = normalize(candidate_rows(raw_ref, first + k, per_step))
            gradient = unnormalize_grad(unit, inverse, gradient)
            for j in range(depth):
                raw_ref[j, pl.ds(first + k, pieces, stride=per_step), :] = gradient[
                    j * pieces : (j + 1) * pieces, :
                ]

    for j in range(depth):
        block = raw_ref[j].reshape(pieces, per_step, width)
        grad_ref[:, :, j * width : (j + 1) * width] = block.astype(grad_ref.dtype)


def query_side_kernel(
    q_ref, page_ref, weight_ref, rows_ref, raw_ref, unit_ref, share_ref, back_ref
):
    per_step = page_ref.shape[1]
    load_pages(page_ref, raw_ref)
    step = pl.program_id(0)
    step_first = step * per_step

    @pl.when(step == 0)
    def _():
        back_ref[...] = jnp.zeros_like(back_ref)

    @pl.loop(0, per_step // math.gcd(per_step, PER_LOOP))
    def _(turn):
        use = share_into(share_ref, weight_ref, step_first + turn * math.gcd(per_step, PER_LOOP))
        fill(q_ref, raw_ref, unit_ref, turn, per_step, use)
        back_ref[...] += lax.dot_general(
            unit_ref[...],
            share_ref[...],
            (((0,), (0,)), ((), ())),
            preferred_element_type=jnp.float32,
        )

    @pl.when(step == pl.num_programs(0) - 1)
    def _():
        rows_ref[...] = back_ref[...].T


def output_kernel(page_ref, out_ref, raw_ref):
    load_pages(page_ref, raw_ref)
    for c in range(page_ref.shape[1]):
        out_ref[c] = candidate_rows(raw_ref, c, page_ref.shape[1])


def in_page_order(own, width):
    pieces, pages, wide = own.shape
    per_step = math.gcd(pages, PER_STEP)
    patches = pieces * wide // width
    return pl.pallas_call(
        output_kernel,
        grid=(pages // per_step,),
        in_specs=[pl.BlockSpec((pieces, per_step, wide), lambda i: (0, i, 0))],
        out_specs=pl.BlockSpec((per_step, patches, width), lambda i: (i, 0, 0)),
        out_shape=jax.ShapeDtypeStruct((pages, patches, width), jnp.float32),
        scratch_shapes=[pltpu.VMEM((wide // width, pieces * per_step, width), jnp.float32)],
        compiler_params=PARAMS,
        name="page_order",
    )(own)


def over_candidates(
    kernel, name, products, query_rows, fetched, weights, out_spec, out_shape, back, window=None
):
    rows, width = query_rows.shape
    pieces, candidates, wide = fetched.shape
    per_step = math.gcd(candidates, PER_STEP)
    first_step = 0
    if window:
        per_step = math.gcd(*window, per_step)
        first_step, candidates = window[0] // per_step, window[1]
    together = math.gcd(per_step, PER_LOOP)
    patches = pieces * wide // width
    scratch = [
        pltpu.VMEM((wide // width, pieces * per_step, width), jnp.float32),
        pltpu.VMEM((together * patches, width), jnp.bfloat16),
    ]
    if weights:
        scratch.append(pltpu.VMEM((together * patches, rows), jnp.bfloat16))
    if back:
        scratch.append(pltpu.VMEM((width, rows), jnp.float32))
    return pl.pallas_call(
        kernel,
        grid=(candidates // per_step,),
        in_specs=[
            pl.BlockSpec((rows, width), lambda i: (0, 0)),
            pl.BlockSpec((pieces, per_step, wide), lambda i: (0, i + first_step, 0)),
        ]
        + [pl.BlockSpec(table.shape, lambda i: (0, 0)) for table in weights],
        out_specs=out_spec,
        out_shape=out_shape,
        scratch_shapes=scratch,
        cost_estimate=pl.CostEstimate(
            flops=2 * products * candidates * patches * rows * width,
            transcendentals=candidates * patches * rows,
            bytes_accessed=4 * candidates * patches * width,
        ),
        compiler_params=PARAMS,
        name=name,
    )(query_rows, fetched, *weights)


def forward_totals(query_rows, fetched):
    shape = jax.ShapeDtypeStruct((fetched.shape[1], query_rows.shape[0]), jnp.float32)
    spec = pl.BlockSpec(shape.shape, lambda i: (0, 0))
    return over_candidates(
        forward_kernel, "forward_totals", 1, query_rows, fetched, [], spec, shape, False
    )


def page_side(query_rows, fetched, weights, window):
    pieces, candidates, wide = fetched.shape
    per_step = math.gcd(*window, candidates, PER_STEP)
    spec = pl.BlockSpec((pieces, per_step, wide), lambda i: (0, i, 0))
    shape = jax.ShapeDtypeStruct((pieces, window[1], wide), GRAD_TYPE)
    kernel = functools.partial(page_side_kernel, window[0])
    return over_candidates(
        kernel, "page_side", 2, query_rows, fetched, [weights], spec, shape, False, window
    )


def query_side(query_rows, fetched, weights):
    spec = pl.BlockSpec(query_rows.shape, lambda i: (0, 0))
    shape = jax.ShapeDtypeStruct(query_rows.shape, jnp.float32)
    return over_candidates(
        query_side_kernel, "query_side", 2, query_rows, fetched, [weights], spec, shape, True
    )


def from_ahead(value, axis, shift):
    devices = lax.axis_size(axis)
    pairs = [((i + shift) % devices, i) for i in range(devices)]
    return lax.ppermute(value, axis, pairs)


ID_ROWS = 8


def local(queries, pages, cand_owner, cand_slot):
    queries_local, tokens, width = queries.shape[1:]
    local_pages, patches = pages.shape[:2]
    owners_count = lax.axis_size("pages")
    group = lax.axis_size("query")
    candidates = cand_owner.shape[1]
    rows_local = queries_local * tokens
    depth = patches // owners_count
    wide = depth * width
    pieces = pages.reshape(local_pages, depth, owners_count, width)
    spread = jnp.transpose(pieces, (2, 1, 0, 3)).reshape(owners_count, depth * local_pages, width)
    wanted = jnp.concatenate([cand_owner[0], cand_slot[0]]).astype(jnp.bfloat16)
    wanted = jnp.pad(wanted[None, :], ((0, ID_ROWS - 1), (0, width - 2 * candidates)))
    wanted = jnp.broadcast_to(wanted[None], (owners_count, ID_ROWS, width))
    arrived = exchange(jnp.concatenate([spread, wanted], axis=1), "pages")
    tiles = [arrived[:, j * local_pages : (j + 1) * local_pages, :] for j in range(depth)]
    table = jnp.concatenate(tiles, axis=2).reshape(owners_count * local_pages, wide)
    ids = arrived[:, depth * local_pages, : 2 * candidates].astype(jnp.int32)
    asked = ids[:, :candidates] * local_pages + ids[:, candidates:]

    q_unit, q_inv = normalize(queries[0])
    q_round = q_unit.astype(jnp.bfloat16).reshape(rows_local, width)
    query_rows = jnp.concatenate(
        [q_round] + [from_ahead(q_round, "query", k) for k in range(1, group)], axis=0
    )

    page_range = jnp.arange(owners_count * local_pages, dtype=jnp.int32)
    picker = (asked.reshape(-1)[:, None] == page_range[None, :]).astype(jnp.bfloat16)
    served = jnp.dot(picker, table, preferred_element_type=jnp.float32).astype(jnp.bfloat16)
    fetched = exchange(served.reshape(owners_count, candidates, wide), "pages")

    own = forward_totals(query_rows, fetched)
    totals = [own] + [from_ahead(own, "query", k) for k in range(1, group)]
    weights, row_losses = weights_of([totals], [k * rows_local for k in range(group)], tokens)
    losses = row_losses[0, :rows_local].reshape(queries_local, tokens)[:, 0]

    edge = FIRST_CHUNK if candidates > FIRST_CHUNK else candidates // 2
    windows = ((0, edge), (edge, candidates - edge))
    terms = [page_side(query_rows, fetched, weights, windows[0])]
    terms.append(page_side(query_rows, fetched, weights, windows[1]))
    returned = [exchange(part, "pages") for part in terms]
    returned[0], weights = lax.optimization_barrier((returned[0], weights))

    grad_rows = query_side(query_rows, fetched, weights).reshape(group, rows_local, width)
    own_grads = grad_rows[0]
    for k in range(1, group):
        own_grads = own_grads + from_ahead(grad_rows[k], "query", group - k)
    query_grad = unnormalize_grad(
        q_unit, q_inv, own_grads.reshape(queries_local, tokens, width)
    )
    returned[1], query_grad = lax.optimization_barrier((returned[1], query_grad))

    summed = 0.0
    for part, (low, count) in zip(returned, windows):
        rows = asked[:, low : low + count].reshape(-1)
        collector = (page_range[:, None] == rows[None, :]).astype(GRAD_TYPE)
        summed = summed + jnp.dot(
            collector, part.reshape(-1, wide), preferred_element_type=jnp.float32
        )
    own = exchange(summed.astype(OWN_TYPE).reshape(owners_count, local_pages, wide), "pages")
    page_grad = in_page_order(own, width)
    return (losses[None, :], query_grad[None], page_grad)


def solution(mesh):
    return jax.shard_map(
        local,
        mesh=mesh,
        in_specs=(
            P("pages", "query", None, None),
            P("pages", "query", None),
            P("pages", None),
            P("pages", None),
        ),
        out_specs=(P("pages", "query"), P("pages", "query", None, None), P("pages", "query", None)),
        check_vma=False,
    )
```

```python
import functools
import math

import jax
import jax.numpy as jnp
from jax import lax
from jax.experimental import pallas as pl
from jax.experimental.pallas import tpu as pltpu
from jax.sharding import PartitionSpec as P

SHARPNESS = 10.0
INV_TEMP = 20.0
LOSS_SCALE = 256.0
EPSILON = 1e-06
EXP2_SCALE = SHARPNESS * math.log2(math.e)
PER_STEP = 8
PER_LOOP = 4
PARAMS = pltpu.CompilerParams(vmem_limit_bytes=24 << 20)
GRAD_TYPE = jnp.bfloat16
OWN_TYPE = jnp.bfloat16


def exchange(value, axis):
    return lax.all_to_all(value, axis, split_axis=0, concat_axis=0, tiled=True)


def normalize(embeddings):
    values = embeddings.astype(jnp.float32)
    inverse = lax.rsqrt(jnp.sum(values * values, axis=-1, keepdims=True) + EPSILON)
    return (values * inverse, inverse)


def unnormalize_grad(unit_vectors, inverse, gradient):
    return inverse * (
        gradient - unit_vectors * jnp.sum(unit_vectors * gradient, axis=-1, keepdims=True)
    )


def group_sums(values, size):
    lanes = values.shape[1]
    lane = lax.broadcasted_iota(jnp.int32, values.shape, 1)
    step = 1
    while step < size:
        ahead = pltpu.roll(values, lanes - step, 1)
        behind = pltpu.roll(values, step, 1)
        values = values + jnp.where((lane // step) % 2 == 0, ahead, behind)
        step *= 2
    return values


def weights_kernel(tokens, shifts, *refs):
    weight_ref, loss_ref = refs[-2:]
    rows = weight_ref.shape[1]
    group = len(shifts)
    tile = math.gcd(rows // group, 128)
    for start in range(0, rows, tile):
        totals = []
        for first in range(0, len(refs) - 2, group):
            total = None
            for ref, shift in zip(refs[first : first + group], shifts):
                at = (start - shift) % rows
                part = ref[:, at : at + tile]
                total = part if total is None else total + part
            totals.append(total)
        totals = jnp.concatenate(totals, axis=0)
        per_token = jnp.log(totals) / SHARPNESS
        logits = INV_TEMP * (group_sums(per_token, tokens) / tokens)
        exponentials = jnp.exp(logits)
        denominator = jnp.sum(exponentials, axis=0, keepdims=True)
        loss_ref[:, start : start + tile] = jnp.log(denominator) - logits[:1]
        candidate = lax.broadcasted_iota(jnp.int32, totals.shape, 0)
        positive = jnp.where(candidate == 0, 1.0, 0.0)
        scaled = LOSS_SCALE * INV_TEMP / tokens * (exponentials / denominator - positive)
        weight_ref[:, start : start + tile] = scaled / totals


def weights_of(chunks, shifts, tokens):
    rows = chunks[0][0].shape[1]
    candidates = sum(parts[0].shape[0] for parts in chunks)
    return pl.pallas_call(
        functools.partial(weights_kernel, tokens, shifts),
        out_shape=[
            jax.ShapeDtypeStruct((candidates, rows), jnp.float32),
            jax.ShapeDtypeStruct((1, rows), jnp.float32),
        ],
        compiler_params=PARAMS,
        name="weights",
    )(*[part for parts in chunks for part in parts])


def row_chunk(rows):
    return 256 if rows % 256 == 0 else rows


def load_pages(page_ref, raw_ref):
    pieces, per_step, _ = page_ref.shape
    depth, rows, width = raw_ref.shape
    for j in range(depth):
        block = page_ref[:, :, j * width : (j + 1) * width].astype(jnp.float32)
        raw_ref[j] = block.reshape(rows, width)


def candidate_rows(raw_ref, c, per_step):
    depth, rows, _ = raw_ref.shape
    parts = [raw_ref[j, pl.ds(c, rows // per_step, stride=per_step), :] for j in range(depth)]
    return jnp.concatenate(parts, axis=0)


def prepare(raw_ref, unit_ref, k, c, per_step):
    unit, inverse = normalize(candidate_rows(raw_ref, c, per_step))
    patches = unit.shape[0]
    unit_ref[k * patches : (k + 1) * patches, :] = unit.astype(jnp.bfloat16)
    return unit, inverse


def exponentials_of(unit_block, row_block):
    scores = lax.dot_general(
        unit_block, row_block, (((1,), (1,)), ((), ())), preferred_element_type=jnp.float32
    )
    return jnp.exp2(scores * EXP2_SCALE)


def fill(q_ref, raw_ref, unit_ref, turn, per_step, use):
    rows = q_ref.shape[0]
    chunk = row_chunk(rows)
    together = math.gcd(per_step, PER_LOOP)
    patches = unit_ref.shape[0] // together
    first = turn * together
    for k in range(together):
        prepare(raw_ref, unit_ref, k, first + k, per_step)
    for start in range(0, rows, chunk):
        block = q_ref[start : start + chunk, :]
        for k in range(together):
            values = exponentials_of(unit_ref[k * patches : (k + 1) * patches, :], block)
            use(k, patches, pl.ds(start, chunk), values)
    return together, patches, first


def share_into(share_ref, weight_ref, row):
    def use(k, patches, columns, values):
        share = weight_ref[pl.ds(row + k, 1), columns] * values
        share_ref[k * patches : (k + 1) * patches, columns] = share.astype(jnp.bfloat16)

    return use


def forward_kernel(q_ref, page_ref, totals_ref, raw_ref, unit_ref):
    per_step = page_ref.shape[1]
    load_pages(page_ref, raw_ref)
    step_first = pl.program_id(0) * per_step
    together = math.gcd(per_step, PER_LOOP)

    @pl.loop(0, per_step // together)
    def _(turn):
        def use(k, patches, columns, values):
            row = pl.ds(step_first + turn * together + k, 1)
            totals_ref[row, columns] = jnp.sum(values, axis=0, keepdims=True)

        fill(q_ref, raw_ref, unit_ref, turn, per_step, use)


def page_side_kernel(q_ref, page_ref, weight_ref, grad_ref, raw_ref, unit_ref, share_ref):
    per_step = page_ref.shape[1]
    pieces = page_ref.shape[0]
    depth, _, width = raw_ref.shape
    load_pages(page_ref, raw_ref)
    step_first = pl.program_id(0) * per_step

    @pl.loop(0, per_step // math.gcd(per_step, PER_LOOP))
    def _(turn):
        use = share_into(share_ref, weight_ref, step_first + turn * math.gcd(per_step, PER_LOOP))
        together, patches, first = fill(q_ref, raw_ref, unit_ref, turn, per_step, use)
        for k in range(together):
            gradient = jnp.dot(
                share_ref[k * patches : (k + 1) * patches, :],
                q_ref[...],
                preferred_element_type=jnp.float32,
            )
            unit, inverse = normalize(candidate_rows(raw_ref, first + k, per_step))
            gradient = unnormalize_grad(unit, inverse, gradient)
            for j in range(depth):
                raw_ref[j, pl.ds(first + k, pieces, stride=per_step), :] = gradient[
                    j * pieces : (j + 1) * pieces, :
                ]

    for j in range(depth):
        block = raw_ref[j].reshape(pieces, per_step, width)
        grad_ref[:, :, j * width : (j + 1) * width] = block.astype(grad_ref.dtype)


def query_side_kernel(
    q_ref, page_ref, weight_ref, rows_ref, raw_ref, unit_ref, share_ref, back_ref
):
    per_step = page_ref.shape[1]
    load_pages(page_ref, raw_ref)
    step = pl.program_id(0)
    step_first = step * per_step

    @pl.when(step == 0)
    def _():
        back_ref[...] = jnp.zeros_like(back_ref)

    @pl.loop(0, per_step // math.gcd(per_step, PER_LOOP))
    def _(turn):
        use = share_into(share_ref, weight_ref, step_first + turn * math.gcd(per_step, PER_LOOP))
        fill(q_ref, raw_ref, unit_ref, turn, per_step, use)
        back_ref[...] += lax.dot_general(
            unit_ref[...],
            share_ref[...],
            (((0,), (0,)), ((), ())),
            preferred_element_type=jnp.float32,
        )

    @pl.when(step == pl.num_programs(0) - 1)
    def _():
        rows_ref[...] = back_ref[...].T


def output_kernel(page_ref, out_ref, raw_ref):
    load_pages(page_ref, raw_ref)
    for c in range(page_ref.shape[1]):
        out_ref[c] = candidate_rows(raw_ref, c, page_ref.shape[1])


def in_page_order(own, width):
    pieces, pages, wide = own.shape
    per_step = math.gcd(pages, PER_STEP)
    patches = pieces * wide // width
    return pl.pallas_call(
        output_kernel,
        grid=(pages // per_step,),
        in_specs=[pl.BlockSpec((pieces, per_step, wide), lambda i: (0, i, 0))],
        out_specs=pl.BlockSpec((per_step, patches, width), lambda i: (i, 0, 0)),
        out_shape=jax.ShapeDtypeStruct((pages, patches, width), jnp.float32),
        scratch_shapes=[pltpu.VMEM((wide // width, pieces * per_step, width), jnp.float32)],
        compiler_params=PARAMS,
        name="page_order",
    )(own)


def over_candidates(
    kernel, name, products, query_rows, fetched, weights, out_spec, out_shape, back
):
    rows, width = query_rows.shape
    pieces, candidates, wide = fetched.shape
    per_step = math.gcd(candidates, PER_STEP)
    together = math.gcd(per_step, PER_LOOP)
    patches = pieces * wide // width
    scratch = [
        pltpu.VMEM((wide // width, pieces * per_step, width), jnp.float32),
        pltpu.VMEM((together * patches, width), jnp.bfloat16),
    ]
    if weights:
        scratch.append(pltpu.VMEM((together * patches, rows), jnp.bfloat16))
    if back:
        scratch.append(pltpu.VMEM((width, rows), jnp.float32))
    return pl.pallas_call(
        kernel,
        grid=(candidates // per_step,),
        in_specs=[
            pl.BlockSpec((rows, width), lambda i: (0, 0)),
            pl.BlockSpec((pieces, per_step, wide), lambda i: (0, i, 0)),
        ]
        + [pl.BlockSpec(table.shape, lambda i: (0, 0)) for table in weights],
        out_specs=out_spec,
        out_shape=out_shape,
        scratch_shapes=scratch,
        cost_estimate=pl.CostEstimate(
            flops=2 * products * candidates * patches * rows * width,
            transcendentals=candidates * patches * rows,
            bytes_accessed=4 * candidates * patches * width,
        ),
        compiler_params=PARAMS,
        name=name,
    )(query_rows, fetched, *weights)


def forward_totals(query_rows, fetched):
    shape = jax.ShapeDtypeStruct((fetched.shape[1], query_rows.shape[0]), jnp.float32)
    spec = pl.BlockSpec(shape.shape, lambda i: (0, 0))
    return over_candidates(
        forward_kernel, "forward_totals", 1, query_rows, fetched, [], spec, shape, False
    )


def page_side(query_rows, fetched, weights):
    pieces, candidates, wide = fetched.shape
    per_step = math.gcd(candidates, PER_STEP)
    spec = pl.BlockSpec((pieces, per_step, wide), lambda i: (0, i, 0))
    shape = jax.ShapeDtypeStruct(fetched.shape, GRAD_TYPE)
    return over_candidates(
        page_side_kernel, "page_side", 2, query_rows, fetched, [weights], spec, shape, False
    )


def query_side(query_rows, fetched, weights):
    spec = pl.BlockSpec(query_rows.shape, lambda i: (0, 0))
    shape = jax.ShapeDtypeStruct(query_rows.shape, jnp.float32)
    return over_candidates(
        query_side_kernel, "query_side", 2, query_rows, fetched, [weights], spec, shape, True
    )


def from_ahead(value, axis, shift):
    devices = lax.axis_size(axis)
    pairs = [((i + shift) % devices, i) for i in range(devices)]
    return lax.ppermute(value, axis, pairs)


ID_ROWS = 8


def local(queries, pages, cand_owner, cand_slot):
    queries_local, tokens, width = queries.shape[1:]
    local_pages, patches = pages.shape[:2]
    owners_count = lax.axis_size("pages")
    group = lax.axis_size("query")
    candidates = cand_owner.shape[1]
    rows_local = queries_local * tokens
    depth = patches // owners_count
    wide = depth * width
    pieces = pages.reshape(local_pages, depth, owners_count, width)
    spread = jnp.transpose(pieces, (2, 1, 0, 3)).reshape(owners_count, depth * local_pages, width)
    wanted = jnp.concatenate([cand_owner[0], cand_slot[0]]).astype(jnp.bfloat16)
    wanted = jnp.pad(wanted[None, :], ((0, ID_ROWS - 1), (0, width - 2 * candidates)))
    wanted = jnp.broadcast_to(wanted[None], (owners_count, ID_ROWS, width))
    arrived = exchange(jnp.concatenate([spread, wanted], axis=1), "pages")
    tiles = [arrived[:, j * local_pages : (j + 1) * local_pages, :] for j in range(depth)]
    table = jnp.concatenate(tiles, axis=2).reshape(owners_count * local_pages, wide)
    ids = arrived[:, depth * local_pages, : 2 * candidates].astype(jnp.int32)
    asked = ids[:, :candidates] * local_pages + ids[:, candidates:]

    q_unit, q_inv = normalize(queries[0])
    q_round = q_unit.astype(jnp.bfloat16).reshape(rows_local, width)
    query_rows = jnp.concatenate(
        [q_round] + [from_ahead(q_round, "query", k) for k in range(1, group)], axis=0
    )

    page_range = jnp.arange(owners_count * local_pages, dtype=jnp.int32)
    picker = (asked.reshape(-1)[:, None] == page_range[None, :]).astype(jnp.bfloat16)
    served = jnp.dot(picker, table, preferred_element_type=jnp.float32).astype(jnp.bfloat16)
    fetched = exchange(served.reshape(owners_count, candidates, wide), "pages")

    own = forward_totals(query_rows, fetched)
    totals = [own] + [from_ahead(own, "query", k) for k in range(1, group)]
    weights, row_losses = weights_of([totals], [k * rows_local for k in range(group)], tokens)
    losses = row_losses[0, :rows_local].reshape(queries_local, tokens)[:, 0]

    returned = exchange(page_side(query_rows, fetched, weights), "pages")

    grad_rows = query_side(query_rows, fetched, weights).reshape(group, rows_local, width)
    own_grads = grad_rows[0]
    for k in range(1, group):
        own_grads = own_grads + from_ahead(grad_rows[k], "query", group - k)
    query_grad = unnormalize_grad(
        q_unit, q_inv, own_grads.reshape(queries_local, tokens, width)
    )
    returned, query_grad = lax.optimization_barrier((returned, query_grad))

    collector = (page_range[:, None] == asked.reshape(-1)[None, :]).astype(GRAD_TYPE)
    summed = jnp.dot(collector, returned.reshape(-1, wide), preferred_element_type=jnp.float32)
    own = exchange(summed.astype(OWN_TYPE).reshape(owners_count, local_pages, wide), "pages")
    page_grad = in_page_order(own, width)
    return (losses[None, :], query_grad[None], page_grad)


def solution(mesh):
    return jax.shard_map(
        local,
        mesh=mesh,
        in_specs=(
            P("pages", "query", None, None),
            P("pages", "query", None),
            P("pages", None),
            P("pages", None),
        ),
        out_specs=(P("pages", "query"), P("pages", "query", None, None), P("pages", "query", None)),
        check_vma=False,
    )
```

```python
import functools
import math

import jax
import jax.numpy as jnp
from jax import lax
from jax.experimental import pallas as pl
from jax.experimental.pallas import tpu as pltpu
from jax.sharding import PartitionSpec as P

SHARPNESS = 10.0
INV_TEMP = 20.0
LOSS_SCALE = 256.0
EPSILON = 1e-06
EXP2_SCALE = SHARPNESS * math.log2(math.e)
PER_STEP = 8
PER_LOOP = 8
EARLY = 16
PARAMS = pltpu.CompilerParams(vmem_limit_bytes=24 << 20)
GRAD_TYPE = jnp.bfloat16
OWN_TYPE = jnp.bfloat16


def exchange(value, axis):
    return lax.all_to_all(value, axis, split_axis=0, concat_axis=0, tiled=True)


def normalize(embeddings):
    values = embeddings.astype(jnp.float32)
    inverse = lax.rsqrt(jnp.sum(values * values, axis=-1, keepdims=True) + EPSILON)
    return (values * inverse, inverse)


def unnormalize_grad(unit_vectors, inverse, gradient):
    return inverse * (
        gradient - unit_vectors * jnp.sum(unit_vectors * gradient, axis=-1, keepdims=True)
    )


def group_sums(values, size):
    lanes = values.shape[1]
    lane = lax.broadcasted_iota(jnp.int32, values.shape, 1)
    step = 1
    while step < size:
        ahead = pltpu.roll(values, lanes - step, 1)
        behind = pltpu.roll(values, step, 1)
        values = values + jnp.where((lane // step) % 2 == 0, ahead, behind)
        step *= 2
    return values


def weights_kernel(tokens, shifts, *refs):
    weight_ref, loss_ref = refs[-2:]
    rows = weight_ref.shape[1]
    group = len(shifts)
    tile = math.gcd(rows // group, 128)
    for start in range(0, rows, tile):
        totals = []
        for first in range(0, len(refs) - 2, group):
            total = None
            for ref, shift in zip(refs[first : first + group], shifts):
                at = (start - shift) % rows
                part = ref[:, at : at + tile]
                total = part if total is None else total + part
            totals.append(total)
        totals = jnp.concatenate(totals, axis=0)
        per_token = jnp.log(totals) / SHARPNESS
        logits = INV_TEMP * (group_sums(per_token, tokens) / tokens)
        exponentials = jnp.exp(logits)
        denominator = jnp.sum(exponentials, axis=0, keepdims=True)
        loss_ref[:, start : start + tile] = jnp.log(denominator) - logits[:1]
        candidate = lax.broadcasted_iota(jnp.int32, totals.shape, 0)
        positive = jnp.where(candidate == 0, 1.0, 0.0)
        scaled = LOSS_SCALE * INV_TEMP / tokens * (exponentials / denominator - positive)
        weight_ref[:, start : start + tile] = scaled / totals


def weights_of(chunks, shifts, tokens):
    rows = chunks[0][0].shape[1]
    candidates = sum(parts[0].shape[0] for parts in chunks)
    return pl.pallas_call(
        functools.partial(weights_kernel, tokens, shifts),
        out_shape=[
            jax.ShapeDtypeStruct((candidates, rows), jnp.float32),
            jax.ShapeDtypeStruct((1, rows), jnp.float32),
        ],
        compiler_params=PARAMS,
        name="weights",
    )(*[part for parts in chunks for part in parts])


def row_chunk(rows):
    return 256 if rows % 256 == 0 else rows


def load_pages(page_ref, raw_ref):
    pieces, per_step, _ = page_ref.shape
    depth, rows, width = raw_ref.shape
    for j in range(depth):
        block = page_ref[:, :, j * width : (j + 1) * width].astype(jnp.float32)
        raw_ref[j] = block.reshape(rows, width)


def candidate_rows(raw_ref, c, per_step):
    depth, rows, _ = raw_ref.shape
    parts = [raw_ref[j, pl.ds(c, rows // per_step, stride=per_step), :] for j in range(depth)]
    return jnp.concatenate(parts, axis=0)


def prepare(raw_ref, unit_ref, k, c, per_step):
    unit, inverse = normalize(candidate_rows(raw_ref, c, per_step))
    patches = unit.shape[0]
    unit_ref[k * patches : (k + 1) * patches, :] = unit.astype(jnp.bfloat16)
    return unit, inverse


def exponentials_of(unit_block, row_block):
    scores = lax.dot_general(
        unit_block, row_block, (((1,), (1,)), ((), ())), preferred_element_type=jnp.float32
    )
    return jnp.exp2(scores * EXP2_SCALE)


def fill(q_ref, raw_ref, unit_ref, turn, per_step, use):
    rows = q_ref.shape[0]
    chunk = row_chunk(rows)
    together = math.gcd(per_step, PER_LOOP)
    patches = unit_ref.shape[0] // together
    first = turn * together
    for k in range(together):
        prepare(raw_ref, unit_ref, k, first + k, per_step)
    for start in range(0, rows, chunk):
        block = q_ref[start : start + chunk, :]
        for k in range(together):
            values = exponentials_of(unit_ref[k * patches : (k + 1) * patches, :], block)
            use(k, patches, pl.ds(start, chunk), values)
    return together, patches, first


def share_into(share_ref, weight_ref, row):
    def use(k, patches, columns, values):
        share = weight_ref[pl.ds(row + k, 1), columns] * values
        share_ref[k * patches : (k + 1) * patches, columns] = share.astype(jnp.bfloat16)

    return use


def forward_kernel(q_ref, page_ref, totals_ref, raw_ref, unit_ref):
    per_step = page_ref.shape[1]
    load_pages(page_ref, raw_ref)
    step_first = pl.program_id(0) * per_step
    together = math.gcd(per_step, PER_LOOP)

    @pl.loop(0, per_step // together)
    def _(turn):
        def use(k, patches, columns, values):
            row = pl.ds(step_first + turn * together + k, 1)
            totals_ref[row, columns] = jnp.sum(values, axis=0, keepdims=True)

        fill(q_ref, raw_ref, unit_ref, turn, per_step, use)


def page_side_kernel(q_ref, page_ref, weight_ref, grad_ref, raw_ref, unit_ref, share_ref):
    per_step = page_ref.shape[1]
    pieces = page_ref.shape[0]
    depth, _, width = raw_ref.shape
    load_pages(page_ref, raw_ref)
    step_first = pl.program_id(0) * per_step

    @pl.loop(0, per_step // math.gcd(per_step, PER_LOOP))
    def _(turn):
        use = share_into(share_ref, weight_ref, step_first + turn * math.gcd(per_step, PER_LOOP))
        together, patches, first = fill(q_ref, raw_ref, unit_ref, turn, per_step, use)
        for k in range(together):
            gradient = jnp.dot(
                share_ref[k * patches : (k + 1) * patches, :],
                q_ref[...],
                preferred_element_type=jnp.float32,
            )
            unit, inverse = normalize(candidate_rows(raw_ref, first + k, per_step))
            gradient = unnormalize_grad(unit, inverse, gradient)
            for j in range(depth):
                raw_ref[j, pl.ds(first + k, pieces, stride=per_step), :] = gradient[
                    j * pieces : (j + 1) * pieces, :
                ]

    for j in range(depth):
        block = raw_ref[j].reshape(pieces, per_step, width)
        grad_ref[:, :, j * width : (j + 1) * width] = block.astype(grad_ref.dtype)


def query_side_kernel(
    q_ref, page_ref, weight_ref, rows_ref, raw_ref, unit_ref, share_ref, back_ref
):
    per_step = page_ref.shape[1]
    load_pages(page_ref, raw_ref)
    step = pl.program_id(0)
    step_first = step * per_step

    @pl.when(step == 0)
    def _():
        back_ref[...] = jnp.zeros_like(back_ref)

    @pl.loop(0, per_step // math.gcd(per_step, PER_LOOP))
    def _(turn):
        use = share_into(share_ref, weight_ref, step_first + turn * math.gcd(per_step, PER_LOOP))
        fill(q_ref, raw_ref, unit_ref, turn, per_step, use)
        back_ref[...] += lax.dot_general(
            unit_ref[...],
            share_ref[...],
            (((0,), (0,)), ((), ())),
            preferred_element_type=jnp.float32,
        )

    @pl.when(step == pl.num_programs(0) - 1)
    def _():
        rows_ref[...] = back_ref[...].T


def collect_kernel(asked_ref, term_ref, sum_ref):
    shape = (sum_ref.shape[0], asked_ref.shape[1])
    page = lax.broadcasted_iota(jnp.int32, shape, 0) + pl.program_id(0) * shape[0]
    picked = jnp.where(page == asked_ref[...], 1.0, 0.0).astype(term_ref.dtype)
    summed = jnp.dot(picked, term_ref[...], preferred_element_type=jnp.float32)
    sum_ref[...] = summed.astype(sum_ref.dtype)


def sum_by_page(asked, terms, pages):
    rows, wide = terms.shape
    tile = math.gcd(pages, 256)
    return pl.pallas_call(
        collect_kernel,
        grid=(pages // tile,),
        in_specs=[
            pl.BlockSpec((1, rows), lambda i: (0, 0)),
            pl.BlockSpec((rows, wide), lambda i: (0, 0)),
        ],
        out_specs=pl.BlockSpec((tile, wide), lambda i: (i, 0)),
        out_shape=jax.ShapeDtypeStruct((pages, wide), OWN_TYPE),
        compiler_params=PARAMS,
        name="collect",
    )(asked, terms)


def output_kernel(page_ref, out_ref, raw_ref):
    load_pages(page_ref, raw_ref)
    for c in range(page_ref.shape[1]):
        out_ref[c] = candidate_rows(raw_ref, c, page_ref.shape[1])


def in_page_order(own, width):
    pieces, pages, wide = own.shape
    per_step = math.gcd(pages, PER_STEP)
    patches = pieces * wide // width
    return pl.pallas_call(
        output_kernel,
        grid=(pages // per_step,),
        in_specs=[pl.BlockSpec((pieces, per_step, wide), lambda i: (0, i, 0))],
        out_specs=pl.BlockSpec((per_step, patches, width), lambda i: (i, 0, 0)),
        out_shape=jax.ShapeDtypeStruct((pages, patches, width), jnp.float32),
        scratch_shapes=[pltpu.VMEM((wide // width, pieces * per_step, width), jnp.float32)],
        compiler_params=PARAMS,
        name="page_order",
    )(own)


def over_candidates(
    kernel, name, products, query_rows, fetched, weights, out_spec, out_shape, back, window=None
):
    rows, width = query_rows.shape
    pieces, candidates, wide = fetched.shape
    per_step = math.gcd(candidates, PER_STEP)
    first_step = 0
    if window:
        per_step = math.gcd(*window, per_step)
        first_step, candidates = window[0] // per_step, window[1]
    together = math.gcd(per_step, PER_LOOP)
    patches = pieces * wide // width
    scratch = [
        pltpu.VMEM((wide // width, pieces * per_step, width), jnp.float32),
        pltpu.VMEM((together * patches, width), jnp.bfloat16),
    ]
    if weights:
        scratch.append(pltpu.VMEM((together * patches, rows), jnp.bfloat16))
    if back:
        scratch.append(pltpu.VMEM((width, rows), jnp.float32))
    return pl.pallas_call(
        kernel,
        grid=(candidates // per_step,),
        in_specs=[
            pl.BlockSpec((rows, width), lambda i: (0, 0)),
            pl.BlockSpec((pieces, per_step, wide), lambda i: (0, i + first_step, 0)),
        ]
        + [pl.BlockSpec(table.shape, lambda i: (0, 0)) for table in weights],
        out_specs=out_spec,
        out_shape=out_shape,
        scratch_shapes=scratch,
        cost_estimate=pl.CostEstimate(
            flops=2 * products * candidates * patches * rows * width,
            transcendentals=candidates * patches * rows,
            bytes_accessed=4 * candidates * patches * width,
        ),
        compiler_params=PARAMS,
        name=name,
    )(query_rows, fetched, *weights)


def forward_totals(query_rows, fetched, window):
    shape = jax.ShapeDtypeStruct((window[1], query_rows.shape[0]), jnp.float32)
    spec = pl.BlockSpec(shape.shape, lambda i: (0, 0))
    return over_candidates(
        forward_kernel, "forward_totals", 1, query_rows, fetched, [], spec, shape, False, window
    )


def page_side(query_rows, fetched, weights):
    pieces, candidates, wide = fetched.shape
    per_step = math.gcd(candidates, PER_STEP)
    spec = pl.BlockSpec((pieces, per_step, wide), lambda i: (0, i, 0))
    shape = pltpu.HBM(fetched.shape, GRAD_TYPE)
    return over_candidates(
        page_side_kernel, "page_side", 2, query_rows, fetched, [weights], spec, shape, False
    )


def query_side(query_rows, fetched, weights):
    spec = pl.BlockSpec(query_rows.shape, lambda i: (0, 0))
    shape = jax.ShapeDtypeStruct(query_rows.shape, jnp.float32)
    return over_candidates(
        query_side_kernel, "query_side", 2, query_rows, fetched, [weights], spec, shape, True
    )


def from_ahead(value, axis, shift):
    devices = lax.axis_size(axis)
    pairs = [((i + shift) % devices, i) for i in range(devices)]
    return lax.ppermute(value, axis, pairs)


ID_ROWS = 8


def local(queries, pages, cand_owner, cand_slot):
    queries_local, tokens, width = queries.shape[1:]
    local_pages, patches = pages.shape[:2]
    owners_count = lax.axis_size("pages")
    group = lax.axis_size("query")
    candidates = cand_owner.shape[1]
    rows_local = queries_local * tokens
    depth = patches // owners_count
    wide = depth * width
    pieces = pages.reshape(local_pages, depth, owners_count, width)
    spread = jnp.transpose(pieces, (2, 1, 0, 3)).reshape(owners_count, depth * local_pages, width)
    wanted = jnp.concatenate([cand_owner[0], cand_slot[0]]).astype(jnp.bfloat16)
    wanted = jnp.pad(wanted[None, :], ((0, ID_ROWS - 1), (0, width - 2 * candidates)))
    wanted = jnp.broadcast_to(wanted[None], (owners_count, ID_ROWS, width))
    arrived = exchange(jnp.concatenate([spread, wanted], axis=1), "pages")
    tiles = [arrived[:, j * local_pages : (j + 1) * local_pages, :] for j in range(depth)]
    table = jnp.concatenate(tiles, axis=2).reshape(owners_count * local_pages, wide)
    ids = arrived[:, depth * local_pages, : 2 * candidates].astype(jnp.int32)
    asked = ids[:, :candidates] * local_pages + ids[:, candidates:]

    q_unit, q_inv = normalize(queries[0])
    q_round = q_unit.astype(jnp.bfloat16).reshape(rows_local, width)
    query_rows = jnp.concatenate(
        [q_round] + [from_ahead(q_round, "query", k) for k in range(1, group)], axis=0
    )

    page_range = jnp.arange(owners_count * local_pages, dtype=jnp.int32)
    picker = (asked.reshape(-1)[:, None] == page_range[None, :]).astype(jnp.bfloat16)
    served = jnp.dot(picker, table, preferred_element_type=jnp.float32).astype(jnp.bfloat16)
    fetched = exchange(served.reshape(owners_count, candidates, wide), "pages")

    edge = EARLY if candidates > EARLY else candidates // 2
    totals = []
    for window in ((0, edge), (edge, candidates - edge)):
        own = forward_totals(query_rows, fetched, window)
        totals.append([own] + [from_ahead(own, "query", k) for k in range(1, group)])
    weights, row_losses = weights_of(totals, [k * rows_local for k in range(group)], tokens)
    losses = row_losses[0, :rows_local].reshape(queries_local, tokens)[:, 0]

    returned = exchange(page_side(query_rows, fetched, weights), "pages")

    grad_rows = query_side(query_rows, fetched, weights).reshape(group, rows_local, width)
    own_grads = grad_rows[0]
    for k in range(1, group):
        own_grads = own_grads + from_ahead(grad_rows[k], "query", group - k)
    query_grad = unnormalize_grad(
        q_unit, q_inv, own_grads.reshape(queries_local, tokens, width)
    )
    returned, query_grad = lax.optimization_barrier((returned, query_grad))

    summed = sum_by_page(asked.reshape(1, -1), returned.reshape(-1, wide), page_range.shape[0])
    own = exchange(summed.reshape(owners_count, local_pages, wide), "pages")
    page_grad = in_page_order(own, width)
    return (losses[None, :], query_grad[None], page_grad)


def solution(mesh):
    return jax.shard_map(
        local,
        mesh=mesh,
        in_specs=(
            P("pages", "query", None, None),
            P("pages", "query", None),
            P("pages", None),
            P("pages", None),
        ),
        out_specs=(P("pages", "query"), P("pages", "query", None, None), P("pages", "query", None)),
        check_vma=False,
    )
```

```python
import functools
import math

import jax
import jax.numpy as jnp
from jax import lax
from jax.experimental import pallas as pl
from jax.experimental.pallas import tpu as pltpu
from jax.sharding import PartitionSpec as P

SHARPNESS = 10.0
INV_TEMP = 20.0
LOSS_SCALE = 256.0
EPSILON = 1e-06
EXP2_SCALE = SHARPNESS * math.log2(math.e)
PER_STEP = 8
PER_LOOP = 8
PARAMS = pltpu.CompilerParams(vmem_limit_bytes=24 << 20)
GRAD_TYPE = jnp.bfloat16
OWN_TYPE = jnp.float32


def exchange(value, axis):
    return lax.all_to_all(value, axis, split_axis=0, concat_axis=0, tiled=True)


def normalize(embeddings):
    values = embeddings.astype(jnp.float32)
    inverse = lax.rsqrt(jnp.sum(values * values, axis=-1, keepdims=True) + EPSILON)
    return (values * inverse, inverse)


def unnormalize_grad(unit_vectors, inverse, gradient):
    return inverse * (
        gradient - unit_vectors * jnp.sum(unit_vectors * gradient, axis=-1, keepdims=True)
    )


def group_sums(values, size):
    lanes = values.shape[1]
    lane = lax.broadcasted_iota(jnp.int32, values.shape, 1)
    step = 1
    while step < size:
        ahead = pltpu.roll(values, lanes - step, 1)
        behind = pltpu.roll(values, step, 1)
        values = values + jnp.where((lane // step) % 2 == 0, ahead, behind)
        step *= 2
    return values


def weights_kernel(tokens, shifts, *refs):
    weight_ref, loss_ref = refs[-2:]
    rows = weight_ref.shape[1]
    group = len(shifts)
    tile = math.gcd(rows // group, 128)
    for start in range(0, rows, tile):
        totals = []
        for first in range(0, len(refs) - 2, group):
            total = None
            for ref, shift in zip(refs[first : first + group], shifts):
                at = (start - shift) % rows
                part = ref[:, at : at + tile]
                total = part if total is None else total + part
            totals.append(total)
        totals = jnp.concatenate(totals, axis=0)
        per_token = jnp.log(totals) / SHARPNESS
        logits = INV_TEMP * (group_sums(per_token, tokens) / tokens)
        exponentials = jnp.exp(logits)
        denominator = jnp.sum(exponentials, axis=0, keepdims=True)
        loss_ref[:, start : start + tile] = jnp.log(denominator) - logits[:1]
        candidate = lax.broadcasted_iota(jnp.int32, totals.shape, 0)
        positive = jnp.where(candidate == 0, 1.0, 0.0)
        scaled = LOSS_SCALE * INV_TEMP / tokens * (exponentials / denominator - positive)
        weight_ref[:, start : start + tile] = scaled / totals


def weights_of(chunks, shifts, tokens):
    rows = chunks[0][0].shape[1]
    candidates = sum(parts[0].shape[0] for parts in chunks)
    return pl.pallas_call(
        functools.partial(weights_kernel, tokens, shifts),
        out_shape=[
            pltpu.HBM((candidates, rows), jnp.float32),
            jax.ShapeDtypeStruct((1, rows), jnp.float32),
        ],
        compiler_params=PARAMS,
        name="weights",
    )(*[part for parts in chunks for part in parts])


def row_chunk(rows):
    return 256 if rows % 256 == 0 else rows


def load_pages(page_ref, raw_ref):
    pieces, per_step, _ = page_ref.shape
    depth, rows, width = raw_ref.shape
    for j in range(depth):
        block = page_ref[:, :, j * width : (j + 1) * width].astype(jnp.float32)
        raw_ref[j] = block.reshape(rows, width)


def candidate_rows(raw_ref, c, per_step):
    depth, rows, _ = raw_ref.shape
    parts = [raw_ref[j, pl.ds(c, rows // per_step, stride=per_step), :] for j in range(depth)]
    return jnp.concatenate(parts, axis=0)


def prepare(raw_ref, unit_ref, k, c, per_step):
    unit, inverse = normalize(candidate_rows(raw_ref, c, per_step))
    patches = unit.shape[0]
    unit_ref[k * patches : (k + 1) * patches, :] = unit.astype(jnp.bfloat16)
    return unit, inverse


def exponentials_of(unit_block, row_block):
    scores = lax.dot_general(
        unit_block, row_block, (((1,), (1,)), ((), ())), preferred_element_type=jnp.float32
    )
    return jnp.exp2(scores * EXP2_SCALE)


def fill(q_ref, raw_ref, unit_ref, turn, per_step, use):
    rows = q_ref.shape[0]
    chunk = row_chunk(rows)
    together = math.gcd(per_step, PER_LOOP)
    patches = unit_ref.shape[0] // together
    first = turn * together
    for k in range(together):
        prepare(raw_ref, unit_ref, k, first + k, per_step)
    for start in range(0, rows, chunk):
        block = q_ref[start : start + chunk, :]
        for k in range(together):
            values = exponentials_of(unit_ref[k * patches : (k + 1) * patches, :], block)
            use(k, patches, pl.ds(start, chunk), values)
    return together, patches, first


def share_into(share_ref, weight_ref, row):
    def use(k, patches, columns, values):
        share = weight_ref[pl.ds(row + k, 1), columns] * values
        share_ref[k * patches : (k + 1) * patches, columns] = share.astype(jnp.bfloat16)

    return use


def turns(count):
    return pl.loop(0, count) if count > 1 else lambda body: body(0)


def forward_kernel(q_ref, page_ref, totals_ref, raw_ref, unit_ref):
    per_step = page_ref.shape[1]
    load_pages(page_ref, raw_ref)
    step_first = pl.program_id(0) * per_step
    together = math.gcd(per_step, PER_LOOP)

    @turns(per_step // together)
    def _(turn):
        def use(k, patches, columns, values):
            row = pl.ds(step_first + turn * together + k, 1)
            totals_ref[row, columns] = jnp.sum(values, axis=0, keepdims=True)

        fill(q_ref, raw_ref, unit_ref, turn, per_step, use)


def page_side_kernel(q_ref, page_ref, weight_ref, grad_ref, raw_ref, unit_ref, share_ref):
    per_step = page_ref.shape[1]
    pieces = page_ref.shape[0]
    depth, _, width = raw_ref.shape
    load_pages(page_ref, raw_ref)
    step_first = pl.program_id(0) * per_step

    @turns(per_step // math.gcd(per_step, PER_LOOP))
    def _(turn):
        use = share_into(share_ref, weight_ref, step_first + turn * math.gcd(per_step, PER_LOOP))
        together, patches, first = fill(q_ref, raw_ref, unit_ref, turn, per_step, use)
        for k in range(together):
            gradient = jnp.dot(
                share_ref[k * patches : (k + 1) * patches, :],
                q_ref[...],
                preferred_element_type=jnp.float32,
            )
            unit, inverse = normalize(candidate_rows(raw_ref, first + k, per_step))
            gradient = unnormalize_grad(unit, inverse, gradient)
            for j in range(depth):
                raw_ref[j, pl.ds(first + k, pieces, stride=per_step), :] = gradient[
                    j * pieces : (j + 1) * pieces, :
                ]

    for j in range(depth):
        block = raw_ref[j].reshape(pieces, per_step, width)
        grad_ref[:, :, j * width : (j + 1) * width] = block.astype(grad_ref.dtype)


def query_side_kernel(
    q_ref, page_ref, weight_ref, rows_ref, raw_ref, unit_ref, share_ref, back_ref
):
    per_step = page_ref.shape[1]
    load_pages(page_ref, raw_ref)
    step = pl.program_id(0)
    step_first = step * per_step

    @pl.when(step == 0)
    def _():
        back_ref[...] = jnp.zeros_like(back_ref)

    @turns(per_step // math.gcd(per_step, PER_LOOP))
    def _(turn):
        use = share_into(share_ref, weight_ref, step_first + turn * math.gcd(per_step, PER_LOOP))
        fill(q_ref, raw_ref, unit_ref, turn, per_step, use)
        back_ref[...] += lax.dot_general(
            unit_ref[...],
            share_ref[...],
            (((0,), (0,)), ((), ())),
            preferred_element_type=jnp.float32,
        )

    @pl.when(step == pl.num_programs(0) - 1)
    def _():
        rows_ref[...] = back_ref[...].T


def spread_kernel(page_ref, wanted_ref, out_ref, rows_ref):
    local_pages, depth, owners, width = page_ref.shape
    block_rows = out_ref.shape[1]
    for slot in range(local_pages):
        for j in range(depth):
            rows = page_ref[slot, j].astype(jnp.float32)
            rows_ref[pl.ds(j * local_pages + slot, owners, stride=block_rows), :] = rows
    for k in range(depth * local_pages, block_rows):
        ids = jnp.broadcast_to(wanted_ref[...], (owners, width))
        rows_ref[pl.ds(k, owners, stride=block_rows), :] = ids
    out_ref[...] = rows_ref[...].reshape(out_ref.shape).astype(out_ref.dtype)


def spread_of(pieces, wanted):
    local_pages, depth, owners, width = pieces.shape
    block_rows = depth * local_pages + ID_ROWS
    return pl.pallas_call(
        spread_kernel,
        out_shape=pltpu.HBM((owners, block_rows, width), pieces.dtype),
        scratch_shapes=[pltpu.VMEM((owners * block_rows, width), jnp.float32)],
        compiler_params=PARAMS,
        name="spread",
    )(pieces, wanted)


def serve_kernel(candidates, local_pages, arrived_ref, out_ref, table_ref, ids_ref):
    owners, block_rows, width = arrived_ref.shape
    depth = (block_rows - ID_ROWS) // local_pages
    together = out_ref.shape[0]
    step = pl.program_id(0)

    @pl.when(step == 0)
    def _():
        for j in range(depth):
            tile = arrived_ref[:, j * local_pages : (j + 1) * local_pages, :]
            table_ref[:, j * width : (j + 1) * width] = tile.reshape(owners * local_pages, width)

    tail = arrived_ref[pl.ds(step * together, together), depth * local_pages :, :]
    ids_ref[...] = tail.astype(jnp.float32).reshape(together * ID_ROWS, width)
    ids = ids_ref[pl.ds(0, together, stride=ID_ROWS), :].T
    pages = table_ref.shape[0]
    page = lax.broadcasted_iota(jnp.int32, (candidates, pages), 1)
    picked = []
    for d in range(together):
        owner = ids[:candidates, d : d + 1].astype(jnp.int32)
        slot = ids[candidates : 2 * candidates, d : d + 1].astype(jnp.int32)
        asked = owner * local_pages + slot
        picked.append(jnp.where(page == asked, 1.0, 0.0))
    picked = jnp.concatenate(picked, axis=0).astype(table_ref.dtype)
    served = jnp.dot(picked, table_ref[...], preferred_element_type=jnp.float32)
    out_ref[...] = served.astype(out_ref.dtype).reshape(out_ref.shape)


def served_from(arrived, candidates, local_pages):
    owners, block_rows, width = arrived.shape
    wide = (block_rows - ID_ROWS) // local_pages * width
    together = math.gcd(owners, 8)
    return pl.pallas_call(
        functools.partial(serve_kernel, candidates, local_pages),
        grid=(owners // together,),
        in_specs=[pl.BlockSpec(arrived.shape, lambda i: (0, 0, 0))],
        out_specs=pl.BlockSpec((together, candidates, wide), lambda i: (i, 0, 0)),
        out_shape=pltpu.HBM((owners, candidates, wide), arrived.dtype),
        scratch_shapes=[
            pltpu.VMEM((owners * local_pages, wide), arrived.dtype),
            pltpu.VMEM((together * ID_ROWS, width), jnp.float32),
        ],
        compiler_params=PARAMS,
        name="serve",
    )(arrived)


def collect_kernel(asked_ref, term_ref, sum_ref):
    shape = (sum_ref.shape[0], asked_ref.shape[1])
    page = lax.broadcasted_iota(jnp.int32, shape, 0) + pl.program_id(0) * shape[0]
    picked = jnp.where(page == asked_ref[...], 1.0, 0.0).astype(term_ref.dtype)
    summed = jnp.dot(picked, term_ref[...], preferred_element_type=jnp.float32)
    sum_ref[...] = summed.astype(sum_ref.dtype)


def sum_by_page(asked, terms, pages):
    rows, wide = terms.shape
    tile = math.gcd(pages, 256)
    return pl.pallas_call(
        collect_kernel,
        grid=(pages // tile,),
        in_specs=[
            pl.BlockSpec((1, rows), lambda i: (0, 0)),
            pl.BlockSpec((rows, wide), lambda i: (0, 0)),
        ],
        out_specs=pl.BlockSpec((tile, wide), lambda i: (i, 0)),
        out_shape=jax.ShapeDtypeStruct((pages, wide), OWN_TYPE),
        compiler_params=PARAMS,
        name="collect",
    )(asked, terms)


def output_kernel(page_ref, out_ref, raw_ref):
    load_pages(page_ref, raw_ref)
    for c in range(page_ref.shape[1]):
        out_ref[c] = candidate_rows(raw_ref, c, page_ref.shape[1])


def in_page_order(own, width):
    pieces, pages, wide = own.shape
    per_step = math.gcd(pages, PER_STEP)
    patches = pieces * wide // width
    return pl.pallas_call(
        output_kernel,
        grid=(pages // per_step,),
        in_specs=[pl.BlockSpec((pieces, per_step, wide), lambda i: (0, i, 0))],
        out_specs=pl.BlockSpec((per_step, patches, width), lambda i: (i, 0, 0)),
        out_shape=jax.ShapeDtypeStruct((pages, patches, width), jnp.float32),
        scratch_shapes=[pltpu.VMEM((wide // width, pieces * per_step, width), jnp.float32)],
        compiler_params=PARAMS,
        name="page_order",
    )(own)


def over_candidates(
    kernel, name, products, query_rows, fetched, weights, out_spec, out_shape, back, window=None
):
    rows, width = query_rows.shape
    pieces, candidates, wide = fetched.shape
    per_step = math.gcd(candidates, PER_STEP)
    first_step = 0
    if window:
        per_step = math.gcd(*window, per_step)
        first_step, candidates = window[0] // per_step, window[1]
    together = math.gcd(per_step, PER_LOOP)
    patches = pieces * wide // width
    scratch = [
        pltpu.VMEM((wide // width, pieces * per_step, width), jnp.float32),
        pltpu.VMEM((together * patches, width), jnp.bfloat16),
    ]
    if weights:
        scratch.append(pltpu.VMEM((together * patches, rows), jnp.bfloat16))
    if back:
        scratch.append(pltpu.VMEM((width, rows), jnp.float32))
    return pl.pallas_call(
        kernel,
        grid=(candidates // per_step,),
        in_specs=[
            pl.BlockSpec((rows, width), lambda i: (0, 0)),
            pl.BlockSpec((pieces, per_step, wide), lambda i: (0, i + first_step, 0)),
        ]
        + [pl.BlockSpec(table.shape, lambda i: (0, 0)) for table in weights],
        out_specs=out_spec,
        out_shape=out_shape,
        scratch_shapes=scratch,
        cost_estimate=pl.CostEstimate(
            flops=2 * products * candidates * patches * rows * width,
            transcendentals=candidates * patches * rows,
            bytes_accessed=4 * candidates * patches * width,
        ),
        compiler_params=PARAMS,
        name=name,
    )(query_rows, fetched, *weights)


def forward_totals(query_rows, fetched, window):
    shape = jax.ShapeDtypeStruct((window[1], query_rows.shape[0]), jnp.float32)
    spec = pl.BlockSpec(shape.shape, lambda i: (0, 0))
    return over_candidates(
        forward_kernel, "forward_totals", 1, query_rows, fetched, [], spec, shape, False, window
    )


def page_side(query_rows, fetched, weights):
    pieces, candidates, wide = fetched.shape
    per_step = math.gcd(candidates, PER_STEP)
    spec = pl.BlockSpec((pieces, per_step, wide), lambda i: (0, i, 0))
    shape = pltpu.HBM(fetched.shape, GRAD_TYPE)
    return over_candidates(
        page_side_kernel, "page_side", 2, query_rows, fetched, [weights], spec, shape, False
    )


def query_side(query_rows, fetched, weights):
    spec = pl.BlockSpec(query_rows.shape, lambda i: (0, 0))
    shape = jax.ShapeDtypeStruct(query_rows.shape, jnp.float32)
    return over_candidates(
        query_side_kernel, "query_side", 2, query_rows, fetched, [weights], spec, shape, True
    )


def from_ahead(value, axis, shift):
    devices = lax.axis_size(axis)
    pairs = [((i + shift) % devices, i) for i in range(devices)]
    return lax.ppermute(value, axis, pairs)


ID_ROWS = 8


def local(queries, pages, cand_owner, cand_slot):
    queries_local, tokens, width = queries.shape[1:]
    local_pages, patches = pages.shape[:2]
    owners_count = lax.axis_size("pages")
    group = lax.axis_size("query")
    candidates = cand_owner.shape[1]
    rows_local = queries_local * tokens
    depth = patches // owners_count
    wide = depth * width
    pieces = pages.reshape(local_pages, depth, owners_count, width)
    wanted = jnp.concatenate([cand_owner, cand_slot], axis=1).astype(jnp.float32)
    wanted = jnp.pad(wanted, ((0, 0), (0, width - 2 * candidates)))
    arrived = exchange(spread_of(pieces, wanted), "pages")
    ids = arrived[:, depth * local_pages, : 2 * candidates].astype(jnp.int32)
    asked = ids[:, :candidates] * local_pages + ids[:, candidates:]

    q_unit, q_inv = normalize(queries[0])
    q_round = q_unit.astype(jnp.bfloat16).reshape(rows_local, width)
    query_rows = jnp.concatenate(
        [q_round] + [from_ahead(q_round, "query", k) for k in range(1, group)], axis=0
    )

    fetched = exchange(served_from(arrived, candidates, local_pages), "pages")

    own = forward_totals(query_rows, fetched, (0, candidates))
    totals = [own] + [from_ahead(own, "query", k) for k in range(1, group)]
    weights, row_losses = weights_of([totals], [k * rows_local for k in range(group)], tokens)
    losses = row_losses[0, :rows_local].reshape(queries_local, tokens)[:, 0]

    returned = exchange(page_side(query_rows, fetched, weights), "pages")

    grad_rows = query_side(query_rows, fetched, weights).reshape(group, rows_local, width)
    own_grads = grad_rows[0]
    for k in range(1, group):
        own_grads = own_grads + from_ahead(grad_rows[k], "query", group - k)
    query_grad = unnormalize_grad(
        q_unit, q_inv, own_grads.reshape(queries_local, tokens, width)
    )
    returned, query_grad = lax.optimization_barrier((returned, query_grad))

    summed = sum_by_page(asked.reshape(1, -1), returned.reshape(-1, wide), owners_count * local_pages)
    own = exchange(summed.reshape(owners_count, local_pages, wide), "pages")
    page_grad = in_page_order(own, width)
    return (losses[None, :], query_grad[None], page_grad)


def solution(mesh):
    return jax.shard_map(
        local,
        mesh=mesh,
        in_specs=(
            P("pages", "query", None, None),
            P("pages", "query", None),
            P("pages", None),
            P("pages", None),
        ),
        out_specs=(P("pages", "query"), P("pages", "query", None, None), P("pages", "query", None)),
        check_vma=False,
    )
```
